32 devices in a mesh: tm: 8 (over y, x, core), space: 4 (over z).
Axes of the slice: x: 2, y: 2, z: 4, core: 2. Of those that a mesh axis runs over, the one named last changes fastest.
Arguments:
- adjoint_iterate: float32 [64, 16, 32, 128], P('tm', None, 'space'), may hold values from -6 to 6
- innovations: float32 [64, 16, 512], P('tm', None, 'space'), may hold values from -6 to 6
- station_cells: int32 [64, 512], P('tm', 'space'), may hold values from 0 to 1023
- diffusivity: float32 [16, 32, 128], P(None, 'space'), may hold values from 0.01 to 0.08
- wind_x: float32 [16, 32, 128], P(None, 'space'), may hold values from -0.2 to 0.2
- wind_y: float32 [16, 32, 128], P(None, 'space'), may hold values from -0.2 to 0.2
- vertical_mixing: float32 [16, 32, 128], P(None, 'space'), may hold values from 0.01 to 0.1
Outputs:
- updated_iterate: float32 [64, 16, 32, 128], P('tm', None, 'space')
The draws below stay inside these ranges and needn't reach their ends.
Inputs may be any that keep to these rules, and one draw needn't show every extreme that they name: `station_cells`: A station's column within its tile of 8 x 128 columns is numbered x * 128 + y; several stations may share a column.
All inputs are finite; a program needn't handle non-finite values.
Results may differ from the reference program's by a relative error of at most 0.0003.
Values sent between devices are 32-bit elements; how exact they have to be, the bound alone decides.
No kernel may reach another device: no remote copies, remote signals or barrier semaphores. Data moves between devices by JAX's collectives and lax.ppermute only.
A program may use at most 64 MiB of HBM per device.

```python
import math
import jax
import jax.numpy as jnp

LEV = 16
TX = 8
NY = 128
STATIONS = 128
INNER = 4
NX = 32
STEPS = 64
STATIONS_ALL = 512


def with_ends(drawn, stream_key, least, largest):
    place = [jax.random.randint(jax.random.fold_in(stream_key, axis), (), 0, length) for axis, length in enumerate(drawn.shape)]
    widest = drawn.shape.index(max(drawn.shape))
    next_to = place[:widest] + [(place[widest] + 1) % drawn.shape[widest]] + place[widest + 1:]
    return drawn.at[tuple(place)].set(least).at[tuple(next_to)].set(largest)


def block_scale(key, extent, shards, least, high):
    factor_of, own = 1.0, jax.random.fold_in(key, 6)
    for axis_at, parts in shards:
        steps = jnp.exp(jax.random.uniform(jax.random.fold_in(own, axis_at), (parts,), jnp.float32, least / len(shards), high / len(shards)))
        factor_of = factor_of * jnp.repeat(steps, extent[axis_at] // parts).reshape([-1 if axis == axis_at else 1 for axis in range(len(extent))])
    return factor_of


def scatter_about(rng, shape, width, reach, split=(), held_as=jnp.bfloat16):
    drawn = width * jax.random.normal(rng, shape, jnp.float32)
    if split:
        drawn = drawn * block_scale(rng, shape, split, -0.22, 0.18)
    return jnp.clip(drawn, -reach, reach).astype(held_as)


def setup_inputs(seed: int = 0) -> dict:
    key_list = jax.random.split(jax.random.key(seed), 8)
    return {
        "adjoint_iterate": scatter_about(key_list[0], (STEPS, LEV, NX, NY), 1.0, 6.0, ((0, 8), (2, 4)), jnp.float32),
        "innovations": scatter_about(key_list[1], (STEPS, LEV, STATIONS_ALL), 1.0, 6.0, ((0, 8), (2, 4)), jnp.float32),
        "station_cells": with_ends(jax.random.randint(key_list[2], (STEPS, STATIONS_ALL), 0, TX * NY), jax.random.fold_in(key_list[2], 1), 0, (TX * NY) - 1).astype(jnp.int32),
        "diffusivity": jnp.clip(jnp.exp(math.log(0.08) - 2.0794415 * jax.random.uniform(key_list[3], (LEV, NX, NY), jnp.float32) ** block_scale(key_list[3], (LEV, NX, NY), ((1, 4),), -0.2, 0.2)), 0.01, 0.08),
        "wind_x": jnp.clip(jax.random.uniform(key_list[4], (LEV, NX, NY), jnp.float32, -0.2, 0.2) * block_scale(key_list[4], (LEV, NX, NY), ((1, 4),), -0.4, 0.0), -0.2, 0.2),
        "wind_y": jnp.clip(jax.random.uniform(key_list[5], (LEV, NX, NY), jnp.float32, -0.2, 0.2) * block_scale(key_list[5], (LEV, NX, NY), ((1, 4),), -0.4, 0.0), -0.2, 0.2),
        "vertical_mixing": jnp.clip(jnp.exp(math.log(0.1) - 2.3025851 * jax.random.uniform(key_list[6], (LEV, NX, NY), jnp.float32) ** block_scale(key_list[6], (LEV, NX, NY), ((1, 4),), -0.2, 0.2)), 0.01, 0.1),
    }


circ_alpha = 0.1


def transfer_rates(diffusivity, wind_x, wind_y, vertical_mixing):
    east_rate = diffusivity + jnp.maximum(-wind_x, 0.0)
    west_rate = diffusivity + jnp.maximum(wind_x, 0.0)
    north_rate = diffusivity + jnp.maximum(-wind_y, 0.0)
    south_rate = diffusivity + jnp.maximum(wind_y, 0.0)
    return jnp.stack([east_rate, west_rate, north_rate, south_rate, vertical_mixing, vertical_mixing])


def apply_transpose(padded, rates_pad, retained):
    center = padded[..., 1:-1, 1:-1, 1:-1]
    summed = retained * center
    summed = summed + rates_pad[0, 1:-1, :-2, 1:-1] * padded[..., 1:-1, :-2, 1:-1]
    summed = summed + rates_pad[1, 1:-1, 2:, 1:-1] * padded[..., 1:-1, 2:, 1:-1]
    summed = summed + rates_pad[2, 1:-1, 1:-1, :-2] * padded[..., 1:-1, 1:-1, :-2]
    summed = summed + rates_pad[3, 1:-1, 1:-1, 2:] * padded[..., 1:-1, 1:-1, 2:]
    summed = summed + rates_pad[4, :-2, 1:-1, 1:-1] * padded[..., :-2, 1:-1, 1:-1]
    summed = summed + rates_pad[5, 2:, 1:-1, 1:-1] * padded[..., 2:, 1:-1, 1:-1]
    return summed


def reference(adjoint_iterate, innovations, station_cells, diffusivity, wind_x, wind_y, vertical_mixing):
    rate_fields = transfer_rates(diffusivity, wind_x, wind_y, vertical_mixing)
    retained = 1.0 - jnp.sum(rate_fields, axis=0)
    rates_pad = jnp.pad(rate_fields, ((0, 0), (1, 1), (1, 1), (1, 1)))
    tile_base = (jnp.arange(STATIONS_ALL, dtype=jnp.int32) // STATIONS) * (TX * NY)
    global_cells = (station_cells + tile_base[None, :]).astype(jnp.int32)

    def scatter_step(cell_ids, values):
        return jnp.zeros((LEV, NX * NY), jnp.float32).at[:, cell_ids].add(values)

    forcing = jax.vmap(scatter_step)(global_cells, innovations).reshape(STEPS, LEV, NX, NY)
    following = jnp.concatenate([adjoint_iterate[1:], jnp.zeros_like(adjoint_iterate[:1])], axis=0)
    following_pad = jnp.pad(following, ((0, 0), (1, 1), (1, 1), (1, 1)))
    residual = forcing - adjoint_iterate + apply_transpose(following_pad, rates_pad, retained)
    log_beta = math.log(circ_alpha) / STEPS
    step_index = jnp.arange(STEPS, dtype=jnp.float32)
    scaled = residual * jnp.exp(-step_index * log_beta)[:, None, None, None]
    spectrum = jnp.fft.fft(scaled, axis=0)
    source = jnp.stack([jnp.real(spectrum), jnp.imag(spectrum)])
    angles = step_index * (2.0 * math.pi / STEPS)
    cos_freq = jnp.cos(angles)[:, None, None, None]
    sin_freq = jnp.sin(angles)[:, None, None, None]
    beta_step = math.exp(log_beta)
    iterate = source
    for sweep_index in range(INNER):
        padded = jnp.pad(iterate, ((0, 0), (0, 0), (1, 1), (1, 1), (1, 1)))
        applied = apply_transpose(padded, rates_pad, retained)
        real_part = source[0] + beta_step * (cos_freq * applied[0] - sin_freq * applied[1])
        imag_part = source[1] + beta_step * (sin_freq * applied[0] + cos_freq * applied[1])
        iterate = jnp.stack([real_part, imag_part])
    restored = jnp.real(jnp.fft.ifft(iterate[0] + 1j * iterate[1], axis=0))
    correction = restored * jnp.exp(step_index * log_beta)[:, None, None, None]
    return adjoint_iterate + correction
```

```python
import jax
import jax.numpy as jnp
from jax import lax
from jax.experimental import pallas as pl
from jax.experimental.pallas import tpu as pltpu
from jax.sharding import PartitionSpec as P

LEV = 16
TX = 8
NY = 128
STEPS_DEV = 8
SWEEPS = 5
HALO = SWEEPS - 1
NEXT = SWEEPS
FNEXT = SWEEPS - 1
OWN = STEPS_DEV - NEXT
XW = TX + 2 * HALO
FT = 16

circ_alpha = 0.1

T_LAM = NEXT * LEV * TX
T_INN = T_LAM + FNEXT * LEV
T_ROWS = T_INN + 8

Z1_LAM = OWN * SWEEPS * LEV
Z1_RATE = Z1_LAM + 4 * HALO * LEV
Z1_INN = Z1_RATE + 7 * LEV
Z1_ROWS = Z1_INN + 8

Z2_LAM = NEXT * SWEEPS * LEV
Z2_INN = Z2_LAM + FNEXT * LEV
Z2_ROWS = Z2_INN + 8


def east(diff, wind):
    return diff + jnp.maximum(-wind, 0.0)


def west(diff, wind):
    return diff + jnp.maximum(wind, 0.0)


def column(ref, base, col, half):
    return ref[pl.ds(base + half * 8 * TX + col, 8, stride=TX), :]


def edge_columns(lam_ref, steps, diff_ref, wx_ref, up_ref, down_ref):
    for step in range(steps[0], steps[1]):
        slot = step - steps[0]
        for half in range(2):
            for place in range(SWEEPS):
                row = (slot * SWEEPS + place) * LEV + 8 * half
                col = TX - SWEEPS + place
                up = column(lam_ref, step * LEV * TX, col, half)
                if place == 0:
                    up = up * east(column(diff_ref, 0, col, half), column(wx_ref, 0, col, half))
                up_ref[row : row + 8, :] = up
                down = column(lam_ref, step * LEV * TX, place, half)
                if place == SWEEPS - 1:
                    down = down * west(column(diff_ref, 0, place, half), column(wx_ref, 0, place, half))
                down_ref[row : row + 8, :] = down


def pack_first(lam_ref, inn_ref, cell_ref, diff_ref, wx_ref, wy_ref, vm_ref, t_ref, up_ref, down_ref):
    t_ref[0:T_LAM, :] = lam_ref[0:T_LAM, :]
    t_ref[T_LAM:T_INN, :] = inn_ref[0 : FNEXT * LEV, :]
    cells = cell_ref[...].astype(jnp.float32)
    t_ref[T_INN:T_ROWS, :] = cells
    edge_columns(lam_ref, (NEXT, STEPS_DEV), diff_ref, wx_ref, up_ref, down_ref)
    for index, ref in enumerate((diff_ref, wx_ref, wy_ref, vm_ref)):
        for place in range(HALO):
            for half in range(2):
                row = Z1_LAM + (index * HALO + place) * LEV + 8 * half
                up_ref[row : row + 8, :] = column(ref, 0, TX - HALO + place, half)
                down_ref[row : row + 8, :] = column(ref, 0, place, half)
    for ref in (up_ref, down_ref):
        ref[Z1_RATE:Z1_INN, :] = inn_ref[LEV : 8 * LEV, :]
        ref[Z1_INN:Z1_ROWS, :] = cells


def pack_second(t_ref, diff_ref, wx_ref, up_ref, down_ref):
    edge_columns(t_ref, (0, NEXT), diff_ref, wx_ref, up_ref, down_ref)
    for ref in (up_ref, down_ref):
        ref[Z2_LAM:Z2_ROWS, :] = t_ref[T_LAM:T_ROWS, :]


def sweep_kernel(
    scale_ref, lam_ref, inn_ref, cell_ref, diff_ref, wx_ref, wy_ref, vm_ref, t_ref, l1_ref, r1_ref, l2_ref, r2_ref,
    out_ref, za_ref, zb_ref, f_ref, ret_ref, e_ref, w_ref, n_ref, s_ref, v_ref, val_ref, cel_ref,
):
    wrap = scale_ref[0]
    first = scale_ref[1]
    extra = scale_ref[2]
    lane = lax.broadcasted_iota(jnp.int32, (8, NY), 1)

    zero = jnp.zeros((8, NY), jnp.float32)
    for edge in range(2):
        base = edge * (LEV + 1) * XW
        for part in range(XW // 8):
            v_ref[base + 8 * part : base + 8 * part + 8, :] = zero
    for at in range(XW):
        for half in range(2):
            fields = []
            for index, ref in enumerate((diff_ref, wx_ref, wy_ref, vm_ref)):
                if at < HALO:
                    row = Z1_LAM + (index * HALO + at) * LEV + 8 * half
                    fields.append(l1_ref[row : row + 8, :])
                elif at < HALO + TX:
                    fields.append(column(ref, 0, at - HALO, half))
                else:
                    row = Z1_LAM + (index * HALO + at - HALO - TX) * LEV + 8 * half
                    fields.append(r1_ref[row : row + 8, :])
            diff, wind_x, wind_y, mixing = fields
            e_rate, w_rate = east(diff, wind_x), west(diff, wind_x)
            n_rate, s_rate = east(diff, wind_y), west(diff, wind_y)
            rows = pl.ds(8 * half * XW + at, 8, stride=XW)
            ret_ref[rows, :] = 1.0 - (e_rate + w_rate + n_rate + s_rate + mixing + mixing)
            e_ref[rows, :] = e_rate
            w_ref[rows, :] = w_rate
            n_ref[rows, :] = jnp.where(lane == 0, 0.0, pltpu.roll(n_rate, 1, 1))
            s_ref[rows, :] = jnp.where(lane == NY - 1, 0.0, pltpu.roll(s_rate, NY - 1, 1))
            v_ref[pl.ds((8 * half + 1) * XW + at, 8, stride=XW), :] = mixing

    for ref in (za_ref, zb_ref):
        for edge in range(2):
            base = edge * (LEV + 1) * XW * 8
            for part in range(XW):
                ref[base + 8 * part : base + 8 * part + 8, :] = zero

    def factor(slot):
        return None if slot < OWN else (first if slot == OWN else wrap)

    def scaled(value, amount):
        return value if amount is None else value * amount

    def place_level(lev, carry):
        for slot in range(STEPS_DEV):
            if slot < OWN:
                row = pl.multiple_of(((slot + NEXT) * LEV + lev) * TX, 8)
                value = lam_ref[pl.ds(row, 8), :]
            else:
                row = pl.multiple_of(((slot - OWN) * LEV + lev) * TX, 8)
                value = t_ref[pl.ds(row, 8), :]
            za_ref[pl.ds(((lev + 1) * XW + HALO) * 8 + slot, 8, stride=8), :] = scaled(value, factor(slot))
        return carry

    lax.fori_loop(0, LEV, place_level, 0)

    def halo_rows(slot, place, half):
        if slot < OWN:
            return 0, (slot * SWEEPS + place) * LEV + 8 * half
        return 1, ((slot - OWN) * SWEEPS + place) * LEV + 8 * half

    for slot in range(STEPS_DEV):
        for half in range(2):
            for place in range(HALO):
                which, row = halo_rows(slot, place + 1, half)
                value = (l1_ref, l2_ref)[which][row : row + 8, :]
                za_ref[pl.ds(((8 * half + 1) * XW + place) * 8 + slot, 8, stride=XW * 8), :] = scaled(value, factor(slot))
                which, row = halo_rows(slot, place, half)
                value = (r1_ref, r2_ref)[which][row : row + 8, :]
                at = HALO + TX + place
                za_ref[pl.ds(((8 * half + 1) * XW + at) * 8 + slot, 8, stride=XW * 8), :] = scaled(value, factor(slot))

    val_ref[0, 0 : 8 * LEV, :] = inn_ref[...]
    cel_ref[0, 0:8, :] = cell_ref[...]
    val_ref[0, 8 * LEV : 12 * LEV, :] = t_ref[T_LAM:T_INN, :] * wrap
    cel_ref[0, 8:16, :] = t_ref[T_INN:T_ROWS, :].astype(jnp.int32)
    for tile, (one, two) in enumerate(((l1_ref, l2_ref), (r1_ref, r2_ref))):
        val_ref[tile + 1, 0:LEV, :] = jnp.zeros((LEV, NY), jnp.float32)
        val_ref[tile + 1, LEV : 8 * LEV, :] = one[Z1_RATE:Z1_INN, :]
        cel_ref[tile + 1, 0:8, :] = one[Z1_INN:Z1_ROWS, :].astype(jnp.int32)
        val_ref[tile + 1, 8 * LEV : 12 * LEV, :] = two[Z2_LAM:Z2_INN, :] * wrap
        cel_ref[tile + 1, 8:16, :] = two[Z2_INN:Z2_ROWS, :].astype(jnp.int32)

    row_y = lax.broadcasted_iota(jnp.int32, (NY, NY), 0)

    def scatter_step(step, carry):
        for tile in range(3):
            value = val_ref[tile, pl.ds(pl.multiple_of(step * LEV, LEV), LEV), :]
            cell = cel_ref[tile, pl.ds(step, 1), :]
            cell_x = lax.shift_right_logical(cell, 7)
            cell_y = cell & (NY - 1)
            high = value.astype(jnp.bfloat16)
            rest = value - high.astype(jnp.float32)
            mid = rest.astype(jnp.bfloat16)
            low = (rest - mid.astype(jnp.float32)).astype(jnp.bfloat16)
            hot_y = jnp.where(row_y == cell_y, 1.0, 0.0).astype(jnp.bfloat16)
            columns = ((0, TX), (TX - HALO, TX), (0, HALO))[tile]
            blocks = []
            for x in range(*columns):
                hot_x = jnp.broadcast_to(jnp.where(cell_x == x, 1.0, 0.0), (LEV, NY)).astype(jnp.bfloat16)
                blocks.append(jnp.concatenate([high * hot_x, mid * hot_x, low * hot_x], axis=1))
            left = jnp.concatenate(blocks, axis=0)
            right = jnp.concatenate([hot_y, hot_y, hot_y], axis=1)
            placed = lax.dot_general(
                left, right, (((1,), (1,)), ((), ())), preferred_element_type=jnp.float32
            )
            start = (HALO, 0, HALO + TX)[tile]
            for index in range(columns[1] - columns[0]):
                for half in range(2):
                    row = index * LEV + 8 * half
                    f_ref[pl.ds((8 * half * XW + start + index) * FT + step, 8, stride=XW * FT), :] = placed[row : row + 8, :]
        return carry

    lax.fori_loop(0, STEPS_DEV + FNEXT, scatter_step, 0)

    for slot in range(STEPS_DEV):
        for half in range(2):
            for at, place, pair in ((0, 0, (l1_ref, l2_ref)), (XW - 1, SWEEPS - 1, (r1_ref, r2_ref))):
                which, row = halo_rows(slot, place, half)
                value = scaled(pair[which][row : row + 8, :], factor(slot))
                rows = pl.ds((8 * half * XW + at) * FT + HALO + slot, 8, stride=XW * FT)
                f_ref[rows, :] = f_ref[rows, :] + value

    @pl.when(extra != 0.0)
    def _():
        for lev in range(LEV):
            rows = pl.ds((lev * XW + HALO) * FT + STEPS_DEV, 8, stride=FT)
            f_ref[rows, :] = f_ref[rows, :] - t_ref[lev * TX : lev * TX + 8, :] * extra
        for half in range(2):
            for place in range(HALO):
                for at, row, ref in (
                    (place, halo_rows(OWN, place + 1, half)[1], l2_ref),
                    (HALO + TX + place, halo_rows(OWN, place, half)[1], r2_ref),
                ):
                    rows = pl.ds((8 * half * XW + at) * FT + STEPS_DEV, 8, stride=XW * FT)
                    f_ref[rows, :] = f_ref[rows, :] - ref[row : row + 8, :] * extra

    def spread(ref, row):
        return jnp.broadcast_to(ref[pl.ds(row, 1), :], (8, NY))

    buffers = (za_ref, zb_ref)
    for sweep in range(SWEEPS):
        source, target = buffers[sweep % 2], buffers[(sweep + 1) % 2]
        offset = HALO - sweep

        def level(lev, carry, source=source, target=target, offset=offset, sweep=sweep):
            def state(up, at):
                return source[pl.ds(pl.multiple_of(((lev + 1 + up) * XW + at) * 8, 8), 8), :]

            for at in range(sweep, XW - sweep):
                row = lev * XW + at
                centre = state(0, at)
                total = f_ref[pl.ds(row * FT + offset, 8), :] + spread(ret_ref, row) * centre
                if at > 0:
                    total = total + spread(e_ref, row - 1) * state(0, at - 1)
                if at < XW - 1:
                    total = total + spread(w_ref, row + 1) * state(0, at + 1)
                total = total + spread(n_ref, row) * pltpu.roll(centre, 1, 1)
                total = total + spread(s_ref, row) * pltpu.roll(centre, NY - 1, 1)
                total = total + spread(v_ref, row) * state(-1, at)
                total = total + spread(v_ref, row + 2 * XW) * state(1, at)
                if sweep < SWEEPS - 1:
                    target[pl.ds(pl.multiple_of(((lev + 1) * XW + at) * 8, 8), 8), :] = total
                else:
                    out_ref[pl.ds(lev * TX + at - HALO, 8, stride=LEV * TX), :] = total
            return carry

        lax.fori_loop(0, LEV, level, 0)


def vmem(count):
    return [pl.BlockSpec(memory_space=pltpu.VMEM)] * count


def rows_of(count):
    return jax.ShapeDtypeStruct((count, NY), jnp.float32)


def body(adjoint_iterate, innovations, station_cells, diffusivity, wind_x, wind_y, vertical_mixing):
    time_parts = lax.axis_size("tm")
    tiles = lax.axis_size("space")
    lam = adjoint_iterate.reshape(STEPS_DEV * LEV * TX, NY)
    inn = innovations.reshape(STEPS_DEV * LEV, NY)
    fields = [field.reshape(LEV * TX, NY) for field in (diffusivity, wind_x, wind_y, vertical_mixing)]

    ahead = [((i + 1) % time_parts, i) for i in range(time_parts)]
    upward = [(i, i + 1) for i in range(tiles - 1)]
    downward = [(i + 1, i) for i in range(tiles - 1)]

    pay_t, pay_up, pay_down = pl.pallas_call(
        pack_first,
        out_shape=(rows_of(T_ROWS), rows_of(Z1_ROWS), rows_of(Z1_ROWS)),
        in_specs=vmem(7),
        out_specs=tuple(vmem(3)),
        name="pack_first",
    )(lam, inn, station_cells, *fields)
    got_t = lax.ppermute(pay_t, "tm", ahead)
    left_one = lax.ppermute(pay_up, "space", upward)
    right_one = lax.ppermute(pay_down, "space", downward)
    pay_up2, pay_down2 = pl.pallas_call(
        pack_second,
        out_shape=(rows_of(Z2_ROWS), rows_of(Z2_ROWS)),
        in_specs=vmem(3),
        out_specs=tuple(vmem(2)),
        name="pack_second",
    )(got_t, fields[0], fields[1])
    left_two = lax.ppermute(pay_up2, "space", upward)
    right_two = lax.ppermute(pay_down2, "space", downward)

    last = lax.axis_index("tm") == time_parts - 1
    scales = jnp.stack(
        [
            jnp.where(last, circ_alpha, 1.0),
            jnp.where(last, 0.0, 1.0),
            jnp.where(last, circ_alpha, 0.0),
        ]
    ).astype(jnp.float32)

    state_rows = (LEV + 2) * XW * 8
    out = pl.pallas_call(
        sweep_kernel,
        out_shape=rows_of(STEPS_DEV * LEV * TX),
        in_specs=[pl.BlockSpec(memory_space=pltpu.SMEM)] + vmem(12),
        out_specs=vmem(1)[0],
        scratch_shapes=[
            pltpu.VMEM((state_rows, NY), jnp.float32),
            pltpu.VMEM((state_rows, NY), jnp.float32),
            pltpu.VMEM((LEV * XW * FT, NY), jnp.float32),
        ]
        + [pltpu.VMEM((LEV * XW, NY), jnp.float32)] * 5
        + [
            pltpu.VMEM(((LEV + 2) * XW, NY), jnp.float32),
            pltpu.VMEM((3, 12 * LEV, NY), jnp.float32),
            pltpu.VMEM((3, 16, NY), jnp.int32),
        ],
        name="sweeps",
    )(scales, lam, inn, station_cells, *fields, got_t, left_one, right_one, left_two, right_two)
    return out.reshape(STEPS_DEV, LEV, TX, NY)


def solution(mesh):
    in_specs = (
        P("tm", None, "space", None),
        P("tm", None, "space"),
        P("tm", "space"),
        P(None, "space", None),
        P(None, "space", None),
        P(None, "space", None),
        P(None, "space", None),
    )
    out_specs = P("tm", None, "space", None)
    return jax.shard_map(body, mesh=mesh, in_specs=in_specs, out_specs=out_specs, check_vma=False)
```

```python
import jax
import jax.numpy as jnp
from jax import lax
from jax.experimental import pallas as pl
from jax.experimental.pallas import tpu as pltpu
from jax.sharding import PartitionSpec as P

LEV = 16
TX = 8
NY = 128
STEPS_DEV = 8
SWEEPS = 5
HALO = SWEEPS - 1
NEXT = SWEEPS
FNEXT = SWEEPS - 1
OWN = STEPS_DEV - NEXT
XW = TX + 2 * HALO
ZW = XW + 2
STEP = LEV * TX
PLANE = XW * LEV

circ_alpha = 0.1

TAIL = FNEXT * LEV + 8
T_COL = NEXT * LEV
T_ROWS = 2 * TAIL + TX * T_COL
N_LAM = SWEEPS * OWN * LEV
N_RATE = N_LAM + 4 * HALO * LEV
N_EDGE = N_RATE + LEV
N_INN = N_EDGE + 7 * LEV
N_ROWS = N_INN + 8
M_LAM = SWEEPS * T_COL
M_ROWS = M_LAM + TAIL


def toward(diff, wind):
    return diff + jnp.maximum(-wind, 0.0)


def against(diff, wind):
    return diff + jnp.maximum(wind, 0.0)


def column(ref, base, col, half):
    return ref[pl.ds(base + half * 8 * TX + col, 8, stride=TX), :]


def pack_kernel(lam_ref, inn_ref, cell_ref, diff_ref, wx_ref, wy_ref, vm_ref, up_ref, down_ref, t_ref):
    cells = cell_ref[...].astype(jnp.float32)
    rates = (diff_ref, wx_ref, wy_ref, vm_ref)
    for half in range(2):
        for place in range(SWEEPS):
            for slot in range(OWN):
                row = (place * OWN + slot) * LEV + 8 * half
                base = (NEXT + slot) * STEP
                up_ref[row : row + 8, :] = column(lam_ref, base, TX - SWEEPS + place, half)
                down_ref[row : row + 8, :] = column(lam_ref, base, place, half)
        for index, ref in enumerate(rates):
            for place in range(HALO):
                row = N_LAM + (index * HALO + place) * LEV + 8 * half
                up_ref[row : row + 8, :] = column(ref, 0, TX - HALO + place, half)
                down_ref[row : row + 8, :] = column(ref, 0, place, half)
        row = N_RATE + 8 * half
        col = TX - SWEEPS
        up_ref[row : row + 8, :] = toward(column(diff_ref, 0, col, half), column(wx_ref, 0, col, half))
        col = SWEEPS - 1
        down_ref[row : row + 8, :] = against(column(diff_ref, 0, col, half), column(wx_ref, 0, col, half))
    for ref in (up_ref, down_ref):
        ref[N_EDGE:N_INN, :] = inn_ref[LEV : 8 * LEV, :]
        ref[N_INN:N_ROWS, :] = cells
    for half in range(2):
        for col in range(TX):
            for slot in range(NEXT):
                row = TAIL + col * T_COL + slot * LEV + 8 * half
                t_ref[row : row + 8, :] = column(lam_ref, slot * STEP, col, half)
    for base in (0, TAIL + TX * T_COL):
        t_ref[base : base + FNEXT * LEV, :] = inn_ref[0 : FNEXT * LEV, :]
        t_ref[base + FNEXT * LEV : base + TAIL, :] = cells


def place_forcing(value, cell, columns, row_y):
    cell_x = lax.shift_right_logical(cell, 7).astype(jnp.float32)
    cell_y = (cell & (NY - 1)).astype(jnp.float32)
    high = value.astype(jnp.bfloat16)
    rest = value - high.astype(jnp.float32)
    mid = rest.astype(jnp.bfloat16)
    low = (rest - mid.astype(jnp.float32)).astype(jnp.bfloat16)
    spread_x = jnp.broadcast_to(cell_x, (LEV, NY)).astype(jnp.bfloat16)
    spread_y = jnp.broadcast_to(cell_y, (LEV, NY)).astype(jnp.bfloat16)
    zero = jnp.zeros((LEV, NY), jnp.bfloat16)
    one = jnp.ones((LEV, NY), jnp.bfloat16)
    hot_y = jnp.concatenate(
        [jnp.where(row_y[LEV * part : LEV * part + LEV] == spread_y, one, zero) for part in range(NY // LEV)], axis=0
    )
    blocks = []
    for x in range(*columns):
        hot = spread_x == jnp.full((LEV, NY), x, jnp.bfloat16)
        blocks.append(jnp.concatenate([jnp.where(hot, part, zero) for part in (high, mid, low)], axis=1))
    return lax.dot_general(
        jnp.concatenate(blocks, axis=0),
        jnp.concatenate([hot_y, hot_y, hot_y], axis=1),
        (((1,), (1,)), ((), ())),
        preferred_element_type=jnp.float32,
    )


def level_rows():
    return lax.broadcasted_iota(jnp.int32, (NY, NY), 0).astype(jnp.float32).astype(jnp.bfloat16)


LEFT = (TX - HALO, TX)
RIGHT = (0, HALO)


def sweeps(chains, first_chain, za_ref, zb_ref, coef_ref, forcing_rows, store):
    width = chains * LEV
    buffers = (za_ref, zb_ref)
    for sweep in range(SWEEPS):
        source, target = buffers[sweep % 2], buffers[(sweep + 1) % 2]

        def at_column(at, carry, source=source, target=target, sweep=sweep):
            base = pl.multiple_of(at * width, LEV)
            plane = pl.multiple_of((at - 1) * LEV, LEV)
            for half in range(2):
                coef = [coef_ref[pl.ds(kind * PLANE + plane + 8 * half, 8), :] for kind in range(7)]
                for chain in range(chains):
                    row = base + chain * LEV + 8 * half
                    centre = source[pl.ds(row, 8), :]
                    step = first_chain + chain + HALO - sweep
                    ref, start = forcing_rows(step)
                    total = ref[pl.ds(start + plane + 8 * half, 8), :] + coef[0] * centre
                    total = total + coef[1] * source[pl.ds(row - width, 8), :]
                    total = total + coef[2] * source[pl.ds(row + width, 8), :]
                    total = total + coef[3] * pltpu.roll(centre, 1, 1)
                    total = total + coef[4] * pltpu.roll(centre, NY - 1, 1)
                    total = total + coef[5] * source[pl.ds(row - 1, 8), :]
                    total = total + coef[6] * source[pl.ds(row + 1, 8), :]
                    if sweep < SWEEPS - 1:
                        target[pl.ds(row, 8), :] = total
                    else:
                        store(chain, at, half, total)
            return carry

        lax.fori_loop(sweep + 1, ZW - 1 - sweep, at_column, 0)


def early_kernel(
    wrap_ref, lam_ref, inn_ref, cell_ref, diff_ref, wx_ref, wy_ref, vm_ref, t_ref, left_ref, right_ref,
    out_ref, coef_ref, f_ref, fown_ref,
    za_ref, zb_ref,
):
    wrap = wrap_ref[0]
    lane = lax.broadcasted_iota(jnp.int32, (8, NY), 1)
    sub = lax.broadcasted_iota(jnp.int32, (8, NY), 0)
    e_rows, w_rows = {}, {}
    for at in range(XW):
        mixings = []
        for half in range(2):
            fields = []
            for index, ref in enumerate((diff_ref, wx_ref, wy_ref, vm_ref)):
                if HALO <= at < HALO + TX:
                    fields.append(column(ref, 0, at - HALO, half))
                else:
                    side, place = (left_ref, at) if at < HALO else (right_ref, at - HALO - TX)
                    row = N_LAM + (index * HALO + place) * LEV + 8 * half
                    fields.append(side[row : row + 8, :])
            diff, wind_x, wind_y, mixing = fields
            e_rate, w_rate = toward(diff, wind_x), against(diff, wind_x)
            n_rate, s_rate = toward(diff, wind_y), against(diff, wind_y)
            mixings.append(mixing)
            row = at * LEV + 8 * half

            def put(kind, at_row, value):
                coef_ref[kind * PLANE + at_row : kind * PLANE + at_row + 8, :] = value

            put(0, row, 1.0 - (e_rate + w_rate + n_rate + s_rate + mixing + mixing))
            if at < XW - 1:
                put(1, row + LEV, e_rate)
            if at > 0:
                put(2, row - LEV, w_rate)
            put(3, row, jnp.where(lane == 0, 0.0, pltpu.roll(n_rate, 1, 1)))
            put(4, row, jnp.where(lane == NY - 1, 0.0, pltpu.roll(s_rate, NY - 1, 1)))
        row = at * LEV
        down_low, down_high = pltpu.roll(mixings[0], 1, 0), pltpu.roll(mixings[1], 1, 0)
        put(5, row, jnp.where(sub == 0, 0.0, down_low))
        put(5, row + 8, jnp.where(sub == 0, down_low, down_high))
        up_low, up_high = pltpu.roll(mixings[0], 7, 0), pltpu.roll(mixings[1], 7, 0)
        put(6, row, jnp.where(sub == 7, up_high, up_low))
        put(6, row + 8, jnp.where(sub == 7, 0.0, up_high))
    coef_ref[PLANE : PLANE + LEV, :] = left_ref[N_RATE:N_EDGE, :]
    coef_ref[3 * PLANE - LEV : 3 * PLANE, :] = right_ref[N_RATE:N_EDGE, :]

    row_y = level_rows()

    def own_step(step, carry):
        value = inn_ref[pl.ds(pl.multiple_of(step * LEV, LEV), LEV), :]
        placed = place_forcing(value, cell_ref[pl.ds(step, 1), :], (0, TX), row_y)
        f_ref[pl.ds(pl.multiple_of(step * PLANE + HALO * LEV, LEV), TX * LEV), :] = placed
        return carry

    lax.fori_loop(0, STEPS_DEV, own_step, 0)

    def next_step(step, carry):
        value = t_ref[pl.ds(pl.multiple_of(step * LEV, LEV), LEV), :] * wrap
        cell = t_ref[pl.ds(FNEXT * LEV + step, 1), :].astype(jnp.int32)
        fown_ref[pl.ds(pl.multiple_of(step * STEP, STEP), STEP), :] = place_forcing(value, cell, (0, TX), row_y)
        return carry

    lax.fori_loop(0, FNEXT, next_step, 0)

    def side_step(step, carry):
        for ref, columns, start in ((left_ref, LEFT, 0), (right_ref, RIGHT, HALO + TX)):
            value = ref[pl.ds(pl.multiple_of(N_EDGE + (step - 1) * LEV, LEV), LEV), :]
            cell = ref[pl.ds(N_INN + step, 1), :].astype(jnp.int32)
            placed = place_forcing(value, cell, columns, row_y)
            f_ref[pl.ds(pl.multiple_of(step * PLANE + start * LEV, LEV), HALO * LEV), :] = placed
        return carry

    lax.fori_loop(1, STEPS_DEV, side_step, 0)

    block = SWEEPS * OWN * LEV
    za_ref[0:block, :] = left_ref[0:block, :]
    za_ref[block + TX * OWN * LEV : 2 * block + TX * OWN * LEV, :] = right_ref[0:block, :]
    for col in range(TX):
        for slot in range(OWN):
            for half in range(2):
                row = block + (col * OWN + slot) * LEV + 8 * half
                za_ref[row : row + 8, :] = column(lam_ref, (NEXT + slot) * STEP, col, half)

    def store(chain, at, half, total):
        out_ref[pl.ds(chain * STEP + half * 8 * TX + at - SWEEPS, 8, stride=TX), :] = total

    sweeps(OWN, 0, za_ref, zb_ref, coef_ref, lambda step: (f_ref, step * PLANE), store)


def late_kernel(
    scale_ref, early_ref, coef_ref, f_ref, fown_ref, t_ref, left_ref, right_ref,
    out_ref, za_ref, zb_ref, fnext_ref,
):
    wrap, first, extra = scale_ref[0], scale_ref[1], scale_ref[2]
    out_ref[0 : OWN * STEP, :] = early_ref[...]
    for at in range(ZW):
        if at < SWEEPS:
            ref, base = left_ref, at * T_COL
        elif at < SWEEPS + TX:
            ref, base = t_ref, TAIL + (at - SWEEPS) * T_COL
        else:
            ref, base = right_ref, TAIL + (at - SWEEPS - TX) * T_COL
        row = at * T_COL
        za_ref[row : row + LEV, :] = ref[base : base + LEV, :] * first
        za_ref[row + LEV : row + T_COL, :] = ref[base + LEV : base + T_COL, :] * wrap

    row_y = level_rows()

    def side_step(step, carry):
        for ref, base, columns, start in ((left_ref, M_LAM, LEFT, 0), (right_ref, 0, RIGHT, HALO + TX)):
            value = ref[pl.ds(pl.multiple_of(base + step * LEV, LEV), LEV), :] * wrap
            cell = ref[pl.ds(base + FNEXT * LEV + step, 1), :].astype(jnp.int32)
            placed = place_forcing(value, cell, columns, row_y)
            fnext_ref[pl.ds(pl.multiple_of(step * PLANE + start * LEV, LEV), HALO * LEV), :] = placed
        rows = pl.ds(pl.multiple_of(step * PLANE + HALO * LEV, LEV), STEP)
        fnext_ref[rows, :] = fown_ref[pl.ds(pl.multiple_of(step * STEP, STEP), STEP), :]
        return carry

    lax.fori_loop(0, FNEXT, side_step, 0)

    @pl.when(extra != 0.0)
    def _():
        for at in range(XW):
            if at < HALO:
                ref, base = left_ref, (at + 1) * T_COL
            elif at < HALO + TX:
                ref, base = t_ref, TAIL + (at - HALO) * T_COL
            else:
                ref, base = right_ref, TAIL + (at - HALO - TX) * T_COL
            rows = slice(at * LEV, at * LEV + LEV)
            fnext_ref[rows, :] = fnext_ref[rows, :] - ref[base : base + LEV, :] * extra

    def forcing_rows(step):
        return (f_ref, (step - OWN) * PLANE) if step < STEPS_DEV else (fnext_ref, (step - STEPS_DEV) * PLANE)

    def store(chain, at, half, total):
        out_ref[pl.ds((OWN + chain) * STEP + half * 8 * TX + at - SWEEPS, 8, stride=TX), :] = total

    sweeps(NEXT, OWN, za_ref, zb_ref, coef_ref, forcing_rows, store)


def vmem(count):
    return [pl.BlockSpec(memory_space=pltpu.VMEM)] * count


def rows_of(count):
    return jax.ShapeDtypeStruct((count, NY), jnp.float32)


def scratch(count):
    return pltpu.VMEM((count, NY), jnp.float32)


SMEM_SPEC = pl.BlockSpec(memory_space=pltpu.SMEM)


def body(adjoint_iterate, innovations, station_cells, diffusivity, wind_x, wind_y, vertical_mixing):
    time_parts = lax.axis_size("tm")
    tiles = lax.axis_size("space")
    lam = adjoint_iterate.reshape(STEPS_DEV * STEP, NY)
    inn = innovations.reshape(STEPS_DEV * LEV, NY)
    fields = [field.reshape(STEP, NY) for field in (diffusivity, wind_x, wind_y, vertical_mixing)]
    last = lax.axis_index("tm") == time_parts - 1
    scales = jnp.where(
        last, jnp.array([circ_alpha, 0.0, circ_alpha], jnp.float32), jnp.array([1.0, 1.0, 0.0], jnp.float32)
    )

    ahead = [((i + 1) % time_parts, i) for i in range(time_parts)]
    upward = [(i, i + 1) for i in range(tiles - 1)]
    downward = [(i + 1, i) for i in range(tiles - 1)]

    pay_up, pay_down, pay_t = pl.pallas_call(
        pack_kernel,
        out_shape=(rows_of(N_ROWS), rows_of(N_ROWS), rows_of(T_ROWS)),
        in_specs=vmem(7),
        out_specs=tuple(vmem(3)),
        compiler_params=pltpu.CompilerParams(vmem_limit_bytes=8 << 20),
        name="pack",
    )(lam, inn, station_cells, *fields)
    got_t = lax.ppermute(pay_t, "tm", ahead)
    left_one = lax.ppermute(pay_up, "space", upward)
    right_one = lax.ppermute(pay_down, "space", downward)
    left_two = lax.ppermute(got_t[T_ROWS - M_ROWS :], "space", upward)
    right_two = lax.ppermute(got_t[:M_ROWS], "space", downward)

    out_early, coef, forcing, forcing_next = pl.pallas_call(
        early_kernel,
        out_shape=(rows_of(OWN * STEP), rows_of(7 * PLANE), rows_of(STEPS_DEV * PLANE), rows_of(FNEXT * STEP)),
        in_specs=[SMEM_SPEC] + vmem(10),
        out_specs=tuple(vmem(4)),
        scratch_shapes=[scratch(ZW * OWN * LEV), scratch(ZW * OWN * LEV)],
        compiler_params=pltpu.CompilerParams(vmem_limit_bytes=20 << 20),
        cost_estimate=pl.CostEstimate(flops=20_000_000, bytes_accessed=8_000_000, transcendentals=0),
        name="early",
    )(scales, lam, inn, station_cells, *fields, got_t, left_one, right_one)

    out = pl.pallas_call(
        late_kernel,
        out_shape=rows_of(STEPS_DEV * STEP),
        in_specs=[SMEM_SPEC] + vmem(7),
        out_specs=vmem(1)[0],
        scratch_shapes=[scratch(ZW * T_COL), scratch(ZW * T_COL), scratch(FNEXT * PLANE)],
        compiler_params=pltpu.CompilerParams(vmem_limit_bytes=20 << 20),
        cost_estimate=pl.CostEstimate(flops=20_000_000, bytes_accessed=8_000_000, transcendentals=0),
        name="late",
    )(scales, out_early, coef, forcing[OWN * PLANE :], forcing_next, got_t, left_two, right_two)
    return out.reshape(STEPS_DEV, LEV, TX, NY)


def solution(mesh):
    in_specs = (
        P("tm", None, "space", None),
        P("tm", None, "space"),
        P("tm", "space"),
        P(None, "space", None),
        P(None, "space", None),
        P(None, "space", None),
        P(None, "space", None),
    )
    out_specs = P("tm", None, "space", None)
    return jax.shard_map(body, mesh=mesh, in_specs=in_specs, out_specs=out_specs, check_vma=False)
```

```python
import jax
import jax.numpy as jnp
from jax import lax
from jax.experimental import pallas as pl
from jax.experimental.pallas import tpu as pltpu
from jax.sharding import PartitionSpec as P

LEV = 16
TX = 8
NY = 128
STEPS_DEV = 8
SWEEPS = 5
HALO = SWEEPS - 1
NEXT = SWEEPS
FNEXT = SWEEPS - 1
OWN = STEPS_DEV - NEXT
XW = TX + 2 * HALO
ZW = XW + 2
STEP = LEV * TX
PLANE = XW * LEV
BLOCK = 4

circ_alpha = 0.1

TAIL = FNEXT * LEV + 8
T_COL = NEXT * LEV
T_ROWS = 2 * TAIL + TX * T_COL
N_LAM = SWEEPS * OWN * LEV
N_RATE = N_LAM + 4 * HALO * LEV
N_EDGE = N_RATE + LEV
N_INN = N_EDGE + 7 * LEV
N_ROWS = N_INN + 8
M_LAM = SWEEPS * T_COL
M_ROWS = M_LAM + TAIL


def toward(diff, wind):
    return diff + jnp.maximum(-wind, 0.0)


def against(diff, wind):
    return diff + jnp.maximum(wind, 0.0)


def column(ref, base, col, half):
    return ref[pl.ds(base + half * 8 * TX + col, 8, stride=TX), :]


def pack_kernel(
    lam_hbm, inn_hbm, cell_hbm, diff_hbm, wx_hbm, wy_hbm, vm_hbm,
    up_ref, down_ref, t_ref, own_ref,
    lam_ref, inn_ref, cell_ref, diff_ref, wx_ref, wy_ref, vm_ref, sems,
):
    late, soon = pl.ds(NEXT * STEP, OWN * STEP), pl.ds(0, NEXT * STEP)
    pairs = [(lam_hbm.at[late], lam_ref.at[late])]
    pairs += [(diff_hbm, diff_ref), (wx_hbm, wx_ref), (wy_hbm, wy_ref), (vm_hbm, vm_ref)]
    pairs += [(inn_hbm, inn_ref), (cell_hbm, cell_ref), (lam_hbm.at[soon], lam_ref.at[soon])]
    copies = [pltpu.make_async_copy(source, target, sems.at[index]) for index, (source, target) in enumerate(pairs)]
    for copy in copies:
        copy.start()
    for copy in copies[:-1]:
        copy.wait()
    cells = cell_ref[...].astype(jnp.float32)
    rates = (diff_ref, wx_ref, wy_ref, vm_ref)
    for half in range(2):
        for col in range(TX):
            for slot in range(OWN):
                value = column(lam_ref, (NEXT + slot) * STEP, col, half)
                row = slot * LEV + 8 * half
                own_ref[col * OWN * LEV + row : col * OWN * LEV + row + 8, :] = value
                if col >= TX - SWEEPS:
                    start = (col - TX + SWEEPS) * OWN * LEV + row
                    up_ref[start : start + 8, :] = value
                if col < SWEEPS:
                    start = col * OWN * LEV + row
                    down_ref[start : start + 8, :] = value
        for index, ref in enumerate(rates):
            for place in range(HALO):
                row = N_LAM + (index * HALO + place) * LEV + 8 * half
                up_ref[row : row + 8, :] = column(ref, 0, TX - HALO + place, half)
                down_ref[row : row + 8, :] = column(ref, 0, place, half)
        row = N_RATE + 8 * half
        col = TX - SWEEPS
        up_ref[row : row + 8, :] = toward(column(diff_ref, 0, col, half), column(wx_ref, 0, col, half))
        col = SWEEPS - 1
        down_ref[row : row + 8, :] = against(column(diff_ref, 0, col, half), column(wx_ref, 0, col, half))
    for ref in (up_ref, down_ref):
        ref[N_EDGE:N_INN, :] = inn_ref[LEV : 8 * LEV, :]
        ref[N_INN:N_ROWS, :] = cells
    for base in (0, TAIL + TX * T_COL):
        t_ref[base : base + FNEXT * LEV, :] = inn_ref[0 : FNEXT * LEV, :]
        t_ref[base + FNEXT * LEV : base + TAIL, :] = cells
    copies[-1].wait()
    for half in range(2):
        for col in range(TX):
            for slot in range(NEXT):
                row = TAIL + col * T_COL + slot * LEV + 8 * half
                t_ref[row : row + 8, :] = column(lam_ref, slot * STEP, col, half)


def place_forcing(value, cell, columns, row_y):
    cell_x = lax.shift_right_logical(cell, 7).astype(jnp.float32)
    cell_y = (cell & (NY - 1)).astype(jnp.float32)
    high = value.astype(jnp.bfloat16)
    rest = value - high.astype(jnp.float32)
    mid = rest.astype(jnp.bfloat16)
    low = (rest - mid.astype(jnp.float32)).astype(jnp.bfloat16)
    spread_x = jnp.broadcast_to(cell_x, (LEV, NY)).astype(jnp.bfloat16)
    spread_y = jnp.broadcast_to(cell_y, (LEV, NY)).astype(jnp.bfloat16)
    zero = jnp.zeros((LEV, NY), jnp.bfloat16)
    one = jnp.ones((LEV, NY), jnp.bfloat16)
    hot_y = jnp.concatenate(
        [jnp.where(row_y[LEV * part : LEV * part + LEV] == spread_y, one, zero) for part in range(NY // LEV)], axis=0
    )
    blocks = []
    for x in range(*columns):
        hot = spread_x == jnp.full((LEV, NY), x, jnp.bfloat16)
        blocks.append(jnp.concatenate([jnp.where(hot, part, zero) for part in (high, mid, low)], axis=1))
    return lax.dot_general(
        jnp.concatenate(blocks, axis=0),
        jnp.concatenate([hot_y, hot_y, hot_y], axis=1),
        (((1,), (1,)), ((), ())),
        preferred_element_type=jnp.float32,
    )


def level_rows():
    return lax.broadcasted_iota(jnp.int32, (NY, NY), 0).astype(jnp.float32).astype(jnp.bfloat16)


LEFT = (TX - HALO, TX)
RIGHT = (0, HALO)


def sweeps(chains, first_chain, za_ref, zb_ref, coef_ref, own_rows, side_rows, store):
    width = chains * LEV
    buffers = (za_ref, zb_ref)
    for sweep in range(SWEEPS):
        source, target = buffers[sweep % 2], buffers[(sweep + 1) % 2]

        def one_column(at, rows, place, source=source, target=target, sweep=sweep):
            base = at * width
            plane = (at - 1) * LEV
            if not isinstance(at, int):
                base, plane = pl.multiple_of(base, LEV), pl.multiple_of(plane, LEV)
            for half in range(2):
                coef = [coef_ref[pl.ds(kind * PLANE + plane + 8 * half, 8), :] for kind in range(7)]
                for chain in range(chains):
                    row = base + chain * LEV + 8 * half
                    centre = source[pl.ds(row, 8), :]
                    step = first_chain + chain + HALO - sweep
                    ref, start = rows(step, place)
                    west_east = coef[1] * source[pl.ds(row - width, 8), :] + coef[2] * source[pl.ds(row + width, 8), :]
                    along = coef[3] * pltpu.roll(centre, 1, 1) + coef[4] * pltpu.roll(centre, NY - 1, 1)
                    down_up = coef[5] * source[pl.ds(row - 1, 8), :] + coef[6] * source[pl.ds(row + 1, 8), :]
                    total = ref[pl.ds(start + 8 * half, 8), :] + coef[0] * centre
                    total = ((total + west_east) + down_up) + along
                    if sweep < SWEEPS - 1:
                        target[pl.ds(row, 8), :] = total
                    else:
                        store(chain, at, half, total)

        def block(index, carry, one_column=one_column):
            for offset in range(BLOCK):
                place = index * BLOCK + offset
                one_column(SWEEPS + place, own_rows, place)
            return carry

        lax.fori_loop(0, TX // BLOCK, block, 0)
        for offset in range(HALO - sweep):
            one_column(SWEEPS - 1 - offset, side_rows, HALO - 1 - offset)
            one_column(SWEEPS + TX + offset, side_rows, HALO + offset)


def factors(last_ref):
    last = last_ref[0] != 0
    return jnp.where(last, circ_alpha, 1.0), jnp.where(last, 0.0, 1.0), jnp.where(last, circ_alpha, 0.0)


def own_kernel(last_ref, inn_ref, cell_ref, t_ref, f_ref):
    wrap, _, extra = factors(last_ref)
    row_y = level_rows()

    def own_steps(index, carry):
        for offset in range(4):
            step = index * 4 + offset
            value = inn_ref[pl.ds(pl.multiple_of(step * LEV, LEV), LEV), :]
            placed = place_forcing(value, cell_ref[pl.ds(step, 1), :], (0, TX), row_y)
            f_ref[pl.ds(pl.multiple_of(step * STEP, STEP), STEP), :] = placed
        return carry

    lax.fori_loop(0, STEPS_DEV // 4, own_steps, 0)
    for step in range(FNEXT):
        value = t_ref[step * LEV : step * LEV + LEV, :] * wrap
        cell = t_ref[FNEXT * LEV + step : FNEXT * LEV + step + 1, :].astype(jnp.int32)
        start = (STEPS_DEV + step) * STEP
        placed = place_forcing(value, cell, (0, TX), row_y)
        if step == 0:
            for col in range(TX):
                state = t_ref[TAIL + col * T_COL : TAIL + col * T_COL + LEV, :]
                f_ref[start + col * LEV : start + col * LEV + LEV, :] = placed[col * LEV : col * LEV + LEV, :] - state * extra
        else:
            f_ref[start : start + STEP, :] = placed


def early_kernel(
    f_ref, own_ref, diff_ref, wx_ref, wy_ref, vm_ref, left_ref, right_ref,
    out_ref, coef_ref, side_ref,
    za_ref, zb_ref,
):
    lane = lax.broadcasted_iota(jnp.int32, (8, NY), 1)
    sub = lax.broadcasted_iota(jnp.int32, (8, NY), 0)
    for at in range(XW):
        mixings = []

        def put(kind, at_row, value):
            coef_ref[kind * PLANE + at_row : kind * PLANE + at_row + 8, :] = value

        for half in range(2):
            fields = []
            for index, ref in enumerate((diff_ref, wx_ref, wy_ref, vm_ref)):
                if HALO <= at < HALO + TX:
                    fields.append(column(ref, 0, at - HALO, half))
                else:
                    side, place = (left_ref, at) if at < HALO else (right_ref, at - HALO - TX)
                    row = N_LAM + (index * HALO + place) * LEV + 8 * half
                    fields.append(side[row : row + 8, :])
            diff, wind_x, wind_y, mixing = fields
            e_rate, w_rate = toward(diff, wind_x), against(diff, wind_x)
            n_rate, s_rate = toward(diff, wind_y), against(diff, wind_y)
            mixings.append(mixing)
            row = at * LEV + 8 * half
            put(0, row, 1.0 - (e_rate + w_rate + n_rate + s_rate + mixing + mixing))
            if at < XW - 1:
                put(1, row + LEV, e_rate)
            if at > 0:
                put(2, row - LEV, w_rate)
            put(3, row, jnp.where(lane == 0, 0.0, pltpu.roll(n_rate, 1, 1)))
            put(4, row, jnp.where(lane == NY - 1, 0.0, pltpu.roll(s_rate, NY - 1, 1)))
        row = at * LEV
        down_low, down_high = pltpu.roll(mixings[0], 1, 0), pltpu.roll(mixings[1], 1, 0)
        put(5, row, jnp.where(sub == 0, 0.0, down_low))
        put(5, row + 8, jnp.where(sub == 0, down_low, down_high))
        up_low, up_high = pltpu.roll(mixings[0], 7, 0), pltpu.roll(mixings[1], 7, 0)
        put(6, row, jnp.where(sub == 7, up_high, up_low))
        put(6, row + 8, jnp.where(sub == 7, 0.0, up_high))
    coef_ref[PLANE : PLANE + LEV, :] = left_ref[N_RATE:N_EDGE, :]
    coef_ref[3 * PLANE - LEV : 3 * PLANE, :] = right_ref[N_RATE:N_EDGE, :]

    row_y = level_rows()

    def side_step(step, carry):
        for index, (ref, columns) in enumerate(((left_ref, LEFT), (right_ref, RIGHT))):
            value = ref[pl.ds(pl.multiple_of(N_EDGE + (step - 1) * LEV, LEV), LEV), :]
            cell = ref[pl.ds(N_INN + step, 1), :].astype(jnp.int32)
            placed = place_forcing(value, cell, columns, row_y)
            side_ref[pl.ds(pl.multiple_of(step * STEP + index * HALO * LEV, LEV), HALO * LEV), :] = placed
        return carry

    def side_steps(index, carry):
        for offset in range(2):
            side_step(2 + index * 2 + offset, 0)
        return carry

    side_step(1, 0)
    lax.fori_loop(0, 3, side_steps, 0)

    block = SWEEPS * OWN * LEV
    inner = TX * OWN * LEV
    za_ref[0:block, :] = left_ref[0:block, :]
    za_ref[block : block + inner, :] = own_ref[...]
    za_ref[block + inner : 2 * block + inner, :] = right_ref[0:block, :]

    def rows_of_ref(ref):
        return lambda step, place: (ref, step * STEP + place * LEV)

    def store(chain, at, half, total):
        out_ref[pl.ds(chain * STEP + half * 8 * TX + at - SWEEPS, 8, stride=TX), :] = total

    sweeps(OWN, 0, za_ref, zb_ref, coef_ref, rows_of_ref(f_ref), rows_of_ref(side_ref), store)


def late_kernel(
    last_ref, early_ref, coef_ref, f_ref, side_ref, t_ref, left_ref, right_ref,
    out_ref, za_ref, zb_ref, fnext_ref,
):
    wrap, first, extra = factors(last_ref)
    out_ref[0 : OWN * STEP, :] = early_ref[...]
    for at in range(ZW):
        if at < SWEEPS:
            ref, base = left_ref, at * T_COL
        elif at < SWEEPS + TX:
            ref, base = t_ref, TAIL + (at - SWEEPS) * T_COL
        else:
            ref, base = right_ref, TAIL + (at - SWEEPS - TX) * T_COL
        row = at * T_COL
        za_ref[row : row + LEV, :] = ref[base : base + LEV, :] * first
        za_ref[row + LEV : row + T_COL, :] = ref[base + LEV : base + T_COL, :] * wrap

    row_y = level_rows()

    def side_steps(pair, carry):
        for offset in range(2):
            step = pair * 2 + offset
            for index, (ref, base, columns) in enumerate(((left_ref, M_LAM, LEFT), (right_ref, 0, RIGHT))):
                value = ref[pl.ds(pl.multiple_of(base + step * LEV, 8), LEV), :] * wrap
                cell = ref[pl.ds(base + FNEXT * LEV + step, 1), :].astype(jnp.int32)
                placed = place_forcing(value, cell, columns, row_y)
                fnext_ref[pl.ds(pl.multiple_of(step * STEP + index * HALO * LEV, LEV), HALO * LEV), :] = placed
        return carry

    lax.fori_loop(0, FNEXT // 2, side_steps, 0)

    @pl.when(extra != 0.0)
    def _():
        for place in range(2 * HALO):
            ref, base = (left_ref, (place + 1) * T_COL) if place < HALO else (right_ref, TAIL + (place - HALO) * T_COL)
            rows = slice(place * LEV, place * LEV + LEV)
            fnext_ref[rows, :] = fnext_ref[rows, :] - ref[base : base + LEV, :] * extra

    def own_rows(step, place):
        return f_ref, step * STEP + place * LEV

    def side_rows(step, place):
        ref, base = (side_ref, step) if step < STEPS_DEV else (fnext_ref, step - STEPS_DEV)
        return ref, base * STEP + place * LEV

    def store(chain, at, half, total):
        out_ref[pl.ds((OWN + chain) * STEP + half * 8 * TX + at - SWEEPS, 8, stride=TX), :] = total

    sweeps(NEXT, OWN, za_ref, zb_ref, coef_ref, own_rows, side_rows, store)


def vmem(count):
    return [pl.BlockSpec(memory_space=pltpu.VMEM)] * count


def rows_of(count):
    return jax.ShapeDtypeStruct((count, NY), jnp.float32)


def scratch(count):
    return pltpu.VMEM((count, NY), jnp.float32)


SMEM_SPEC = pl.BlockSpec(memory_space=pltpu.SMEM)


def body(adjoint_iterate, innovations, station_cells, diffusivity, wind_x, wind_y, vertical_mixing):
    time_parts = lax.axis_size("tm")
    tiles = lax.axis_size("space")
    lam = adjoint_iterate.reshape(STEPS_DEV * STEP, NY)
    inn = innovations.reshape(STEPS_DEV * LEV, NY)
    fields = [field.reshape(STEP, NY) for field in (diffusivity, wind_x, wind_y, vertical_mixing)]
    last = (lax.axis_index("tm") == time_parts - 1).astype(jnp.int32).reshape(1)

    ahead = [((i + 1) % time_parts, i) for i in range(time_parts)]
    upward = [(i, i + 1) for i in range(tiles - 1)]
    downward = [(i + 1, i) for i in range(tiles - 1)]

    arguments = (lam, inn, station_cells, *fields)
    pay_up, pay_down, pay_t, own = pl.pallas_call(
        pack_kernel,
        out_shape=(rows_of(N_ROWS), rows_of(N_ROWS), rows_of(T_ROWS), rows_of(OWN * STEP)),
        in_specs=[pl.BlockSpec(memory_space=pltpu.HBM)] * 7,
        out_specs=tuple(vmem(4)),
        scratch_shapes=[pltpu.VMEM(value.shape, value.dtype) for value in arguments] + [pltpu.SemaphoreType.DMA((8,))],
        compiler_params=pltpu.CompilerParams(vmem_limit_bytes=8 << 20),
        name="pack",
    )(*[pltpu.with_memory_space_constraint(value, pltpu.HBM) for value in arguments])
    got_t = lax.ppermute(pay_t, "tm", ahead)
    left_one = lax.ppermute(pay_up, "space", upward)
    right_one = lax.ppermute(pay_down, "space", downward)
    left_two = lax.ppermute(got_t[T_ROWS - M_ROWS :], "space", upward)
    right_two = lax.ppermute(got_t[:M_ROWS], "space", downward)

    forcing = pl.pallas_call(
        own_kernel,
        out_shape=rows_of((STEPS_DEV + FNEXT) * STEP),
        in_specs=[SMEM_SPEC] + vmem(3),
        out_specs=vmem(1)[0],
        compiler_params=pltpu.CompilerParams(vmem_limit_bytes=16 << 20),
        cost_estimate=pl.CostEstimate(flops=5_000_000, bytes_accessed=4_000_000, transcendentals=0),
        name="own",
    )(last, inn, station_cells, got_t)
    out_early, coef, side = pl.pallas_call(
        early_kernel,
        out_shape=(rows_of(OWN * STEP), rows_of(7 * PLANE), rows_of(STEPS_DEV * STEP)),
        in_specs=vmem(8),
        out_specs=tuple(vmem(3)),
        scratch_shapes=[scratch(ZW * OWN * LEV), scratch(ZW * OWN * LEV)],
        compiler_params=pltpu.CompilerParams(vmem_limit_bytes=16 << 20),
        cost_estimate=pl.CostEstimate(flops=20_000_000, bytes_accessed=8_000_000, transcendentals=0),
        name="early",
    )(forcing, own, *fields, left_one, right_one)
    out = pl.pallas_call(
        late_kernel,
        out_shape=rows_of(STEPS_DEV * STEP),
        in_specs=[SMEM_SPEC] + vmem(7),
        out_specs=vmem(1)[0],
        scratch_shapes=[scratch(ZW * T_COL), scratch(ZW * T_COL), scratch(FNEXT * STEP)],
        compiler_params=pltpu.CompilerParams(vmem_limit_bytes=16 << 20),
        cost_estimate=pl.CostEstimate(flops=20_000_000, bytes_accessed=8_000_000, transcendentals=0),
        name="late",
    )(last, out_early, coef, forcing, side, got_t, left_two, right_two)
    return out.reshape(STEPS_DEV, LEV, TX, NY)


def solution(mesh):
    in_specs = (
        P("tm", None, "space", None),
        P("tm", None, "space"),
        P("tm", "space"),
        P(None, "space", None),
        P(None, "space", None),
        P(None, "space", None),
        P(None, "space", None),
    )
    out_specs = P("tm", None, "space", None)
    return jax.shard_map(body, mesh=mesh, in_specs=in_specs, out_specs=out_specs, check_vma=False)
```

```python
import jax
import jax.numpy as jnp
from jax import lax
from jax.experimental import pallas as pl
from jax.experimental.pallas import tpu as pltpu
from jax.sharding import PartitionSpec as P

LEV = 16
TX = 8
NY = 128
STEPS_DEV = 8
SWEEPS = 5
HALO = SWEEPS - 1
NEXT = SWEEPS
FNEXT = SWEEPS - 1
OWN = STEPS_DEV - NEXT
XW = TX + 2 * HALO
ZW = XW + 2
STEP = LEV * TX
PLANE = XW * LEV
BLOCK = 4

circ_alpha = 0.1

TAIL = FNEXT * LEV + 8
T_COL = NEXT * LEV
T_ROWS = 2 * TAIL + TX * T_COL
N_LAM = SWEEPS * OWN * LEV
N_RATE = N_LAM + 4 * HALO * LEV
N_EDGE = N_RATE + LEV
N_INN = N_EDGE + 7 * LEV
N_ROWS = N_INN + 8
K_INN = OWN * STEP
K_CELL = K_INN + STEPS_DEV * LEV
K_RATE = K_CELL + 8
K_ROWS = K_RATE + 4 * STEP
M_LAM = SWEEPS * T_COL
M_ROWS = M_LAM + TAIL


def toward(diff, wind):
    return diff + jnp.maximum(-wind, 0.0)


def against(diff, wind):
    return diff + jnp.maximum(wind, 0.0)


def column(ref, base, col, half):
    return ref[pl.ds(base + half * 8 * TX + col, 8, stride=TX), :]


def flags_of(code_ref):
    return [lax.shift_right_logical(code_ref[0], bit) & 1 for bit in range(4)]


def pack_kernel(
    code_ref, lam_hbm, inn_hbm, cell_hbm, diff_hbm, wx_hbm, wy_hbm, vm_hbm,
    here_ref, back_ref, t_ref, keep_ref,
    lam_ref, cell_ref, sems,
):
    late, soon = pl.ds(NEXT * STEP, OWN * STEP), pl.ds(0, NEXT * STEP)
    pairs = [(lam_hbm.at[late], lam_ref.at[late])]
    pairs += [
        (rate, keep_ref.at[pl.ds(K_RATE + index * STEP, STEP)])
        for index, rate in enumerate((diff_hbm, wx_hbm, wy_hbm, vm_hbm))
    ]
    pairs += [(inn_hbm, keep_ref.at[pl.ds(K_INN, STEPS_DEV * LEV)]), (cell_hbm, cell_ref)]
    pairs += [(lam_hbm.at[soon], lam_ref.at[soon])]
    copies = [pltpu.make_async_copy(source, target, sems.at[index]) for index, (source, target) in enumerate(pairs)]
    for copy in copies:
        copy.start()
    odd = flags_of(code_ref)[1]
    for copy in copies[:-1]:
        copy.wait()
    cells = cell_ref[...].astype(jnp.float32)
    keep_ref[K_CELL:K_RATE, :] = cells
    far = TX - SWEEPS
    for ref, first in ((here_ref, far * (1 - odd)), (back_ref, far * odd)):
        rate_first = jnp.where(first == 0, 0, TX - HALO)
        for half in range(2):
            for place in range(SWEEPS):
                for slot in range(OWN):
                    row = (place * OWN + slot) * LEV + 8 * half
                    ref[row : row + 8, :] = column(lam_ref, (NEXT + slot) * STEP, first + place, half)
            for index in range(4):
                for place in range(HALO):
                    row = N_LAM + (index * HALO + place) * LEV + 8 * half
                    ref[row : row + 8, :] = column(keep_ref, K_RATE + index * STEP, rate_first + place, half)
            row = N_RATE + 8 * half
            leaving = toward(column(keep_ref, K_RATE, far, half), column(keep_ref, K_RATE + STEP, far, half))
            place = SWEEPS - 1
            entering = against(column(keep_ref, K_RATE, place, half), column(keep_ref, K_RATE + STEP, place, half))
            ref[row : row + 8, :] = jnp.where(first == 0, entering, leaving)
        ref[N_EDGE:N_INN, :] = keep_ref[K_INN + LEV : K_INN + 8 * LEV, :]
        ref[N_INN:N_ROWS, :] = cells
    for half in range(2):
        for col in range(TX):
            for slot in range(OWN):
                row = (col * OWN + slot) * LEV + 8 * half
                keep_ref[row : row + 8, :] = column(lam_ref, (NEXT + slot) * STEP, col, half)
    for base in (0, TAIL + TX * T_COL):
        t_ref[base : base + FNEXT * LEV, :] = keep_ref[K_INN : K_INN + FNEXT * LEV, :]
        t_ref[base + FNEXT * LEV : base + TAIL, :] = cells
    copies[-1].wait()
    for half in range(2):
        for col in range(TX):
            for slot in range(NEXT):
                row = TAIL + col * T_COL + slot * LEV + 8 * half
                t_ref[row : row + 8, :] = column(lam_ref, slot * STEP, col, half)


def by_side(odd, here_ref, back_ref, left_ref, right_ref):
    for parity, sources in enumerate(((here_ref, back_ref), (back_ref, here_ref))):

        @pl.when(odd == parity)
        def _(sources=sources):
            for source, target in zip(sources, (left_ref, right_ref)):
                target[...] = source[...]


def place_forcing(value, cell, columns, row_y):
    cell_x = lax.shift_right_logical(cell, 7).astype(jnp.float32)
    cell_y = (cell & (NY - 1)).astype(jnp.float32)
    high = value.astype(jnp.bfloat16)
    rest = value - high.astype(jnp.float32)
    mid = rest.astype(jnp.bfloat16)
    low = (rest - mid.astype(jnp.float32)).astype(jnp.bfloat16)
    spread_x = jnp.broadcast_to(cell_x, (LEV, NY)).astype(jnp.bfloat16)
    spread_y = jnp.broadcast_to(cell_y, (LEV, NY)).astype(jnp.bfloat16)
    zero = jnp.zeros((LEV, NY), jnp.bfloat16)
    one = jnp.ones((LEV, NY), jnp.bfloat16)
    hot_y = jnp.concatenate(
        [jnp.where(row_y[LEV * part : LEV * part + LEV] == spread_y, one, zero) for part in range(NY // LEV)], axis=0
    )
    blocks = []
    for x in range(*columns):
        hot = spread_x == jnp.full((LEV, NY), x, jnp.bfloat16)
        blocks.append(jnp.concatenate([jnp.where(hot, part, zero) for part in (high, mid, low)], axis=1))
    return lax.dot_general(
        jnp.concatenate(blocks, axis=0),
        jnp.concatenate([hot_y, hot_y, hot_y], axis=1),
        (((1,), (1,)), ((), ())),
        preferred_element_type=jnp.float32,
    )


def level_rows():
    return lax.broadcasted_iota(jnp.int32, (NY, NY), 0).astype(jnp.float32).astype(jnp.bfloat16)


LEFT = (TX - HALO, TX)
RIGHT = (0, HALO)


def sweeps(chains, first_chain, za_ref, zb_ref, coef_ref, own_rows, side_rows, store):
    width = chains * LEV
    buffers = (za_ref, zb_ref)
    for sweep in range(SWEEPS):
        source, target = buffers[sweep % 2], buffers[(sweep + 1) % 2]

        def one_column(at, rows, place, source=source, target=target, sweep=sweep):
            base = at * width
            plane = (at - 1) * LEV
            if not isinstance(at, int):
                base, plane = pl.multiple_of(base, LEV), pl.multiple_of(plane, LEV)
            for half in range(2):
                coef = [coef_ref[pl.ds(kind * PLANE + plane + 8 * half, 8), :] for kind in range(7)]
                for chain in range(chains):
                    row = base + chain * LEV + 8 * half
                    centre = source[pl.ds(row, 8), :]
                    step = first_chain + chain + HALO - sweep
                    ref, start = rows(step, place)
                    west_east = coef[1] * source[pl.ds(row - width, 8), :] + coef[2] * source[pl.ds(row + width, 8), :]
                    along = coef[3] * pltpu.roll(centre, 1, 1) + coef[4] * pltpu.roll(centre, NY - 1, 1)
                    down_up = coef[5] * source[pl.ds(row - 1, 8), :] + coef[6] * source[pl.ds(row + 1, 8), :]
                    total = ref[pl.ds(start + 8 * half, 8), :] + coef[0] * centre
                    total = ((total + west_east) + down_up) + along
                    if sweep < SWEEPS - 1:
                        target[pl.ds(row, 8), :] = total
                    else:
                        store(chain, at, half, total)

        def block(index, carry, one_column=one_column):
            for offset in range(BLOCK):
                place = index * BLOCK + offset
                one_column(SWEEPS + place, own_rows, place)
            return carry

        lax.fori_loop(0, TX // BLOCK, block, 0)
        for offset in range(HALO - sweep):
            one_column(SWEEPS - 1 - offset, side_rows, HALO - 1 - offset)
            one_column(SWEEPS + TX + offset, side_rows, HALO + offset)


def factors(last):
    last = last != 0
    return jnp.where(last, circ_alpha, 1.0), jnp.where(last, 0.0, 1.0), jnp.where(last, circ_alpha, 0.0)


def own_kernel(code_ref, keep_ref, t_ref, f_ref):
    wrap, _, extra = factors(flags_of(code_ref)[0])
    row_y = level_rows()

    def own_steps(index, carry):
        for offset in range(4):
            step = index * 4 + offset
            value = keep_ref[pl.ds(pl.multiple_of(K_INN + step * LEV, LEV), LEV), :]
            cell = keep_ref[pl.ds(K_CELL + step, 1), :].astype(jnp.int32)
            placed = place_forcing(value, cell, (0, TX), row_y)
            f_ref[pl.ds(pl.multiple_of(step * STEP, STEP), STEP), :] = placed
        return carry

    lax.fori_loop(0, STEPS_DEV // 4, own_steps, 0)
    for step in range(FNEXT):
        value = t_ref[step * LEV : step * LEV + LEV, :] * wrap
        cell = t_ref[FNEXT * LEV + step : FNEXT * LEV + step + 1, :].astype(jnp.int32)
        start = (STEPS_DEV + step) * STEP
        placed = place_forcing(value, cell, (0, TX), row_y)
        if step == 0:
            for col in range(TX):
                state = t_ref[TAIL + col * T_COL : TAIL + col * T_COL + LEV, :]
                f_ref[start + col * LEV : start + col * LEV + LEV, :] = placed[col * LEV : col * LEV + LEV, :] - state * extra
        else:
            f_ref[start : start + STEP, :] = placed


def early_kernel(
    code_ref, f_ref, keep_ref, here_ref, back_ref,
    out_ref, coef_ref, side_ref,
    za_ref, zb_ref, left_ref, right_ref,
):
    _, odd, first_tile, last_tile = flags_of(code_ref)
    by_side(odd, here_ref, back_ref, left_ref, right_ref)
    open_left = jnp.where(first_tile != 0, 0.0, 1.0)
    open_right = jnp.where(last_tile != 0, 0.0, 1.0)
    lane = lax.broadcasted_iota(jnp.int32, (8, NY), 1)
    sub = lax.broadcasted_iota(jnp.int32, (8, NY), 0)
    for at in range(XW):
        mixings = []

        def put(kind, at_row, value):
            coef_ref[kind * PLANE + at_row : kind * PLANE + at_row + 8, :] = value

        for half in range(2):
            fields = []
            for index in range(4):
                if HALO <= at < HALO + TX:
                    fields.append(column(keep_ref, K_RATE + index * STEP, at - HALO, half))
                else:
                    side, place = (left_ref, at) if at < HALO else (right_ref, at - HALO - TX)
                    row = N_LAM + (index * HALO + place) * LEV + 8 * half
                    fields.append(side[row : row + 8, :])
            diff, wind_x, wind_y, mixing = fields
            e_rate, w_rate = toward(diff, wind_x), against(diff, wind_x)
            n_rate, s_rate = toward(diff, wind_y), against(diff, wind_y)
            mixings.append(mixing)
            row = at * LEV + 8 * half
            put(0, row, 1.0 - (e_rate + w_rate + n_rate + s_rate + mixing + mixing))
            if at < XW - 1:
                put(1, row + LEV, e_rate * open_left if at == HALO - 1 else e_rate)
            if at > 0:
                put(2, row - LEV, w_rate * open_right if at == HALO + TX else w_rate)
            put(3, row, jnp.where(lane == 0, 0.0, pltpu.roll(n_rate, 1, 1)))
            put(4, row, jnp.where(lane == NY - 1, 0.0, pltpu.roll(s_rate, NY - 1, 1)))
        row = at * LEV
        down_low, down_high = pltpu.roll(mixings[0], 1, 0), pltpu.roll(mixings[1], 1, 0)
        put(5, row, jnp.where(sub == 0, 0.0, down_low))
        put(5, row + 8, jnp.where(sub == 0, down_low, down_high))
        up_low, up_high = pltpu.roll(mixings[0], 7, 0), pltpu.roll(mixings[1], 7, 0)
        put(6, row, jnp.where(sub == 7, up_high, up_low))
        put(6, row + 8, jnp.where(sub == 7, 0.0, up_high))
    coef_ref[PLANE : PLANE + LEV, :] = left_ref[N_RATE:N_EDGE, :]
    coef_ref[3 * PLANE - LEV : 3 * PLANE, :] = right_ref[N_RATE:N_EDGE, :]

    row_y = level_rows()

    def side_step(step, carry):
        for index, (ref, columns) in enumerate(((left_ref, LEFT), (right_ref, RIGHT))):
            value = ref[pl.ds(pl.multiple_of(N_EDGE + (step - 1) * LEV, LEV), LEV), :]
            cell = ref[pl.ds(N_INN + step, 1), :].astype(jnp.int32)
            placed = place_forcing(value, cell, columns, row_y)
            side_ref[pl.ds(pl.multiple_of(step * STEP + index * HALO * LEV, LEV), HALO * LEV), :] = placed
        return carry

    def side_steps(index, carry):
        for offset in range(2):
            side_step(2 + index * 2 + offset, 0)
        return carry

    side_step(1, 0)
    lax.fori_loop(0, 3, side_steps, 0)

    block = SWEEPS * OWN * LEV
    inner = TX * OWN * LEV
    za_ref[0:block, :] = left_ref[0:block, :]
    za_ref[block : block + inner, :] = keep_ref[0:inner, :]
    za_ref[block + inner : 2 * block + inner, :] = right_ref[0:block, :]

    def rows_of_ref(ref):
        return lambda step, place: (ref, step * STEP + place * LEV)

    def store(chain, at, half, total):
        out_ref[pl.ds(chain * STEP + half * 8 * TX + at - SWEEPS, 8, stride=TX), :] = total

    sweeps(OWN, 0, za_ref, zb_ref, coef_ref, rows_of_ref(f_ref), rows_of_ref(side_ref), store)


def late_kernel(
    code_ref, early_ref, coef_ref, f_ref, side_ref, t_ref, here_ref, back_ref,
    out_ref, za_ref, zb_ref, fnext_ref, left_ref, right_ref,
):
    last, odd = flags_of(code_ref)[:2]
    wrap, first, extra = factors(last)
    by_side(odd, here_ref, back_ref, left_ref, right_ref)
    out_ref[0 : OWN * STEP, :] = early_ref[...]
    for at in range(ZW):
        if at < SWEEPS:
            ref, base = left_ref, at * T_COL
        elif at < SWEEPS + TX:
            ref, base = t_ref, TAIL + (at - SWEEPS) * T_COL
        else:
            ref, base = right_ref, TAIL + (at - SWEEPS - TX) * T_COL
        row = at * T_COL
        za_ref[row : row + LEV, :] = ref[base : base + LEV, :] * first
        za_ref[row + LEV : row + T_COL, :] = ref[base + LEV : base + T_COL, :] * wrap

    row_y = level_rows()

    def side_steps(pair, carry):
        for offset in range(2):
            step = pair * 2 + offset
            for index, (ref, base, columns) in enumerate(((left_ref, M_LAM, LEFT), (right_ref, 0, RIGHT))):
                value = ref[pl.ds(pl.multiple_of(base + step * LEV, 8), LEV), :] * wrap
                cell = ref[pl.ds(base + FNEXT * LEV + step, 1), :].astype(jnp.int32)
                placed = place_forcing(value, cell, columns, row_y)
                fnext_ref[pl.ds(pl.multiple_of(step * STEP + index * HALO * LEV, LEV), HALO * LEV), :] = placed
        return carry

    lax.fori_loop(0, FNEXT // 2, side_steps, 0)

    @pl.when(extra != 0.0)
    def _():
        for place in range(2 * HALO):
            ref, base = (left_ref, (place + 1) * T_COL) if place < HALO else (right_ref, TAIL + (place - HALO) * T_COL)
            rows = slice(place * LEV, place * LEV + LEV)
            fnext_ref[rows, :] = fnext_ref[rows, :] - ref[base : base + LEV, :] * extra

    def own_rows(step, place):
        return f_ref, step * STEP + place * LEV

    def side_rows(step, place):
        ref, base = (side_ref, step) if step < STEPS_DEV else (fnext_ref, step - STEPS_DEV)
        return ref, base * STEP + place * LEV

    def store(chain, at, half, total):
        out_ref[pl.ds((OWN + chain) * STEP + half * 8 * TX + at - SWEEPS, 8, stride=TX), :] = total

    sweeps(NEXT, OWN, za_ref, zb_ref, coef_ref, own_rows, side_rows, store)


def vmem(count):
    return [pl.BlockSpec(memory_space=pltpu.VMEM)] * count


def rows_of(count):
    return jax.ShapeDtypeStruct((count, NY), jnp.float32)


def scratch(count):
    return pltpu.VMEM((count, NY), jnp.float32)


SMEM_SPEC = pl.BlockSpec(memory_space=pltpu.SMEM)


def body(adjoint_iterate, innovations, station_cells, diffusivity, wind_x, wind_y, vertical_mixing):
    time_parts = lax.axis_size("tm")
    tiles = lax.axis_size("space")
    lam = adjoint_iterate.reshape(STEPS_DEV * STEP, NY)
    inn = innovations.reshape(STEPS_DEV * LEV, NY)
    fields = [field.reshape(STEP, NY) for field in (diffusivity, wind_x, wind_y, vertical_mixing)]
    time_rank, tile = lax.axis_index("tm"), lax.axis_index("space")
    odd = time_rank & 1
    code = (time_rank == time_parts - 1) + 2 * odd + 4 * (tile == 0) + 8 * (tile == tiles - 1)
    code = code.astype(jnp.int32).reshape(1)

    ahead = [((i + 1) % time_parts, i) for i in range(time_parts)]

    def neighbours(flip):
        pairs = []
        for part in range(time_parts):
            step = 1 if part % 2 == flip else -1
            for place in range(tiles):
                inside = 0 <= place + step < tiles
                target = part * tiles + place + step if inside else (part ^ 1) * tiles + place
                pairs.append((part * tiles + place, target))
        return pairs

    there, again = neighbours(0), neighbours(1)
    both = ("tm", "space")

    arguments = (lam, inn, station_cells, *fields)
    pay_here, pay_back, pay_t, keep = pl.pallas_call(
        pack_kernel,
        out_shape=(rows_of(N_ROWS), rows_of(N_ROWS), rows_of(T_ROWS), rows_of(K_ROWS)),
        in_specs=[SMEM_SPEC] + [pl.BlockSpec(memory_space=pltpu.HBM)] * 7,
        out_specs=tuple(vmem(4)),
        scratch_shapes=[
            scratch(STEPS_DEV * STEP),
            pltpu.VMEM(station_cells.shape, station_cells.dtype),
            pltpu.SemaphoreType.DMA((8,)),
        ],
        compiler_params=pltpu.CompilerParams(vmem_limit_bytes=8 << 20),
        name="pack",
    )(code, *[pltpu.with_memory_space_constraint(value, pltpu.HBM) for value in arguments])
    got_t = lax.ppermute(pay_t, "tm", ahead)
    here_one = lax.ppermute(pay_here, both, there)
    back_one = lax.ppermute(pay_back, both, again)
    start = (T_ROWS - M_ROWS) * (1 - odd)
    here_two = lax.ppermute(lax.dynamic_slice_in_dim(got_t, start, M_ROWS), both, there)
    back_two = lax.ppermute(lax.dynamic_slice_in_dim(got_t, T_ROWS - M_ROWS - start, M_ROWS), both, again)

    forcing = pl.pallas_call(
        own_kernel,
        out_shape=rows_of((STEPS_DEV + FNEXT) * STEP),
        in_specs=[SMEM_SPEC] + vmem(2),
        out_specs=vmem(1)[0],
        compiler_params=pltpu.CompilerParams(vmem_limit_bytes=16 << 20),
        cost_estimate=pl.CostEstimate(flops=5_000_000, bytes_accessed=4_000_000, transcendentals=0),
        name="own",
    )(code, keep, got_t)
    out_early, coef, side = pl.pallas_call(
        early_kernel,
        out_shape=(rows_of(OWN * STEP), rows_of(7 * PLANE), rows_of(STEPS_DEV * STEP)),
        in_specs=[SMEM_SPEC] + vmem(4),
        out_specs=tuple(vmem(3)),
        scratch_shapes=[scratch(ZW * OWN * LEV), scratch(ZW * OWN * LEV), scratch(N_ROWS), scratch(N_ROWS)],
        compiler_params=pltpu.CompilerParams(vmem_limit_bytes=16 << 20),
        cost_estimate=pl.CostEstimate(flops=20_000_000, bytes_accessed=8_000_000, transcendentals=0),
        name="early",
    )(code, forcing, keep, here_one, back_one)
    out = pl.pallas_call(
        late_kernel,
        out_shape=rows_of(STEPS_DEV * STEP),
        in_specs=[SMEM_SPEC] + vmem(7),
        out_specs=vmem(1)[0],
        scratch_shapes=[scratch(ZW * T_COL), scratch(ZW * T_COL), scratch(FNEXT * STEP), scratch(M_ROWS), scratch(M_ROWS)],
        compiler_params=pltpu.CompilerParams(vmem_limit_bytes=16 << 20),
        cost_estimate=pl.CostEstimate(flops=20_000_000, bytes_accessed=8_000_000, transcendentals=0),
        name="late",
    )(code, out_early, coef, forcing, side, got_t, here_two, back_two)
    return out.reshape(STEPS_DEV, LEV, TX, NY)


def solution(mesh):
    in_specs = (
        P("tm", None, "space", None),
        P("tm", None, "space"),
        P("tm", "space"),
        P(None, "space", None),
        P(None, "space", None),
        P(None, "space", None),
        P(None, "space", None),
    )
    out_specs = P("tm", None, "space", None)
    return jax.shard_map(body, mesh=mesh, in_specs=in_specs, out_specs=out_specs, check_vma=False)
```

```python
import jax
import jax.numpy as jnp
from jax import lax
from jax.experimental import pallas as pl
from jax.experimental.pallas import tpu as pltpu
from jax.sharding import PartitionSpec as P


LEV = 16
TX = 8
NY = 128
STEPS_DEV = 8
SWEEPS = 5
HALO = SWEEPS - 1
NEXT = SWEEPS
FNEXT = SWEEPS - 1
OWN = STEPS_DEV - NEXT
XW = TX + 2 * HALO
ZW = XW + 2
STEP = LEV * TX
PLANE = XW * LEV

circ_alpha = 0.1

PARTS = ((0, 2, 0, 1), (2, 3, 1, 3))
TAILS = tuple(part[3] * LEV + 8 for part in PARTS)
T_BASE = (0, 2 * TAILS[0] + TX * PARTS[0][1] * LEV)
T_ROWS = T_BASE[1] + 2 * TAILS[1] + TX * PARTS[1][1] * LEV
N_INN = SWEEPS * OWN * LEV
N_CELL = N_INN + 7 * LEV
N_RATE = N_CELL + 8
N_EDGE = N_RATE + 4 * HALO * LEV
N_ROWS = N_EDGE + LEV
K_INN = OWN * STEP
K_CELL = K_INN + STEPS_DEV * LEV
K_RATE = K_CELL + 8
K_ROWS = K_RATE + 4 * STEP


def part_rows(part):
    return SWEEPS * PARTS[part][1] * LEV + TAILS[part]


def toward(diff, wind):
    return diff + jnp.maximum(-wind, 0.0)


def against(diff, wind):
    return diff + jnp.maximum(wind, 0.0)


def column(ref, base, col, half):
    return ref[pl.ds(base + half * 8 * TX + col, 8, stride=TX), :]


def flags_of(code_ref):
    return [lax.shift_right_logical(code_ref[0], bit) & 1 for bit in range(4)]


def pack_kernel(
    code_ref, lam_hbm, inn_hbm, cell_hbm, diff_hbm, wx_hbm, wy_hbm, vm_hbm,
    here_ref, back_ref, t_ref, keep_ref,
    lam_ref, cell_ref, sems,
):
    late, soon = pl.ds(NEXT * STEP, OWN * STEP), pl.ds(0, NEXT * STEP)
    pairs = [(lam_hbm.at[late], lam_ref.at[late])]
    pairs += [
        (rate, keep_ref.at[pl.ds(K_RATE + index * STEP, STEP)])
        for index, rate in enumerate((diff_hbm, wx_hbm, wy_hbm, vm_hbm))
    ]
    pairs += [(inn_hbm, keep_ref.at[pl.ds(K_INN, STEPS_DEV * LEV)]), (cell_hbm, cell_ref)]
    pairs += [(lam_hbm.at[soon], lam_ref.at[soon])]
    copies = [pltpu.make_async_copy(source, target, sems.at[index]) for index, (source, target) in enumerate(pairs)]
    for copy in copies:
        copy.start()
    odd = flags_of(code_ref)[1]
    far = TX - SWEEPS
    sides = ((here_ref, far * (1 - odd)), (back_ref, far * odd))
    copies[0].wait()
    for half in range(2):
        for col in range(TX):
            for slot in range(OWN):
                row = (col * OWN + slot) * LEV + 8 * half
                keep_ref[row : row + 8, :] = column(lam_ref, (NEXT + slot) * STEP, col, half)
    for ref, first in sides:
        start = pl.multiple_of(first * (OWN * LEV), LEV)
        ref[0:N_INN, :] = keep_ref[pl.ds(start, N_INN), :]
    for copy in copies[1:5]:
        copy.wait()
    first = sides[0][1]
    rate_first = (TX - HALO) * (1 - odd)
    for half in range(2):
        for index in range(4):
            for place in range(HALO):
                row = N_RATE + (index * HALO + place) * LEV + 8 * half
                here_ref[row : row + 8, :] = column(keep_ref, K_RATE + index * STEP, rate_first + place, half)
        leaving = toward(column(keep_ref, K_RATE, far, half), column(keep_ref, K_RATE + STEP, far, half))
        place = SWEEPS - 1
        entering = against(column(keep_ref, K_RATE, place, half), column(keep_ref, K_RATE + STEP, place, half))
        here_ref[N_EDGE + 8 * half : N_EDGE + 8 * half + 8, :] = jnp.where(odd == 0, leaving, entering)
    for copy in copies[5:7]:
        copy.wait()
    cells = cell_ref[...].astype(jnp.float32)
    keep_ref[K_CELL:K_RATE, :] = cells
    for ref in (here_ref, back_ref):
        ref[N_INN:N_CELL, :] = keep_ref[K_INN + LEV : K_INN + 8 * LEV, :]
        ref[N_CELL:N_RATE, :] = cells
    for (_, states, first_inn, inns), tail, base in zip(PARTS, TAILS, T_BASE):
        for start in (base, base + tail + TX * states * LEV):
            row = K_INN + first_inn * LEV
            t_ref[start : start + inns * LEV, :] = keep_ref[row : row + inns * LEV, :]
            t_ref[start + inns * LEV : start + tail, :] = cells
    copies[7].wait()
    for (first_state, states, _, _), tail, base in zip(PARTS, TAILS, T_BASE):
        for half in range(2):
            for col in range(TX):
                for slot in range(states):
                    row = base + tail + (col * states + slot) * LEV + 8 * half
                    t_ref[row : row + 8, :] = column(lam_ref, (first_state + slot) * STEP, col, half)


def by_side(odd, work, here, back):
    pl.when(odd == 0)(lambda: work(here, back))
    pl.when(odd != 0)(lambda: work(back, here))


def place_forcing(value, cell, columns, row_y):
    cell_x = lax.shift_right_logical(cell, 7).astype(jnp.float32)
    cell_y = (cell & (NY - 1)).astype(jnp.float32)
    high = value.astype(jnp.bfloat16)
    rest = value - high.astype(jnp.float32)
    mid = rest.astype(jnp.bfloat16)
    low = (rest - mid.astype(jnp.float32)).astype(jnp.bfloat16)
    spread_x = jnp.broadcast_to(cell_x, (LEV, NY)).astype(jnp.bfloat16)
    spread_y = jnp.broadcast_to(cell_y, (LEV, NY)).astype(jnp.bfloat16)
    zero = jnp.zeros((LEV, NY), jnp.bfloat16)
    one = jnp.ones((LEV, NY), jnp.bfloat16)
    hot_y = jnp.concatenate(
        [jnp.where(row_y[LEV * part : LEV * part + LEV] == spread_y, one, zero) for part in range(NY // LEV)], axis=0
    )
    blocks = []
    for x in range(*columns):
        hot = spread_x == jnp.full((LEV, NY), x, jnp.bfloat16)
        blocks.append(jnp.concatenate([jnp.where(hot, part, zero) for part in (high, mid, low)], axis=1))
    return lax.dot_general(
        jnp.concatenate(blocks, axis=0),
        jnp.concatenate([hot_y, hot_y, hot_y], axis=1),
        (((1,), (1,)), ((), ())),
        preferred_element_type=jnp.float32,
    )


def level_rows():
    return lax.broadcasted_iota(jnp.int32, (NY, NY), 0).astype(jnp.float32).astype(jnp.bfloat16)


LEFT = (TX - HALO, TX)
RIGHT = (0, HALO)


def sweeps(chains, first_chain, za_ref, zb_ref, coef_ref, own_rows, side_rows, store):
    width = chains * LEV
    buffers = (za_ref, zb_ref)
    for sweep in range(SWEEPS):
        source, target = buffers[sweep % 2], buffers[(sweep + 1) % 2]

        def one_column(at, rows, place, source=source, target=target, sweep=sweep):
            base = at * width
            plane = (at - 1) * LEV
            for half in range(2):
                coef = [coef_ref[pl.ds(kind * PLANE + plane + 8 * half, 8), :] for kind in range(7)]
                for chain in range(chains):
                    row = base + chain * LEV + 8 * half
                    centre = source[pl.ds(row, 8), :]
                    step = first_chain + chain + HALO - sweep
                    ref, start = rows(step, place)
                    west_east = coef[1] * source[pl.ds(row - width, 8), :] + coef[2] * source[pl.ds(row + width, 8), :]
                    along = coef[3] * pltpu.roll(centre, 1, 1) + coef[4] * pltpu.roll(centre, NY - 1, 1)
                    down_up = coef[5] * source[pl.ds(row - 1, 8), :] + coef[6] * source[pl.ds(row + 1, 8), :]
                    total = ref[pl.ds(start + 8 * half, 8), :] + coef[0] * centre
                    total = ((total + west_east) + down_up) + along
                    if sweep < SWEEPS - 1:
                        target[pl.ds(row, 8), :] = total
                    else:
                        store(chain, at, half, total)

        for place in range(TX):
            one_column(SWEEPS + place, own_rows, place)
        for offset in range(HALO - sweep):
            one_column(SWEEPS - 1 - offset, side_rows, HALO - 1 - offset)
            one_column(SWEEPS + TX + offset, side_rows, HALO + offset)


def factors(last):
    last = last != 0
    return jnp.where(last, circ_alpha, 1.0), jnp.where(last, 0.0, 1.0), jnp.where(last, circ_alpha, 0.0)


def own_kernel(keep_ref, f_ref):
    row_y = level_rows()

    def own_steps(index, carry):
        for offset in range(4):
            step = index * 4 + offset
            value = keep_ref[pl.ds(pl.multiple_of(K_INN + step * LEV, LEV), LEV), :]
            cell = keep_ref[pl.ds(K_CELL + step, 1), :].astype(jnp.int32)
            placed = place_forcing(value, cell, (0, TX), row_y)
            f_ref[pl.ds(pl.multiple_of(step * STEP, STEP), STEP), :] = placed
        return carry

    lax.fori_loop(0, STEPS_DEV // 4, own_steps, 0)


def next_kernel(code_ref, t_ref, f_ref):
    wrap, _, extra = factors(flags_of(code_ref)[0])
    row_y = level_rows()
    for (_, _, first_inn, inns), base in zip(PARTS, T_BASE):
        for slot in range(inns):
            step = first_inn + slot
            value = t_ref[base + slot * LEV : base + slot * LEV + LEV, :] * wrap
            row = base + inns * LEV + step
            cell = t_ref[row : row + 1, :].astype(jnp.int32)
            placed = place_forcing(value, cell, (0, TX), row_y)
            if step == 0:
                width = PARTS[0][1] * LEV
                states = [t_ref[TAILS[0] + col * width : TAILS[0] + col * width + LEV, :] for col in range(TX)]
                placed = placed - jnp.concatenate(states, axis=0) * extra
            f_ref[step * STEP : step * STEP + STEP, :] = placed


def early_kernel(
    code_ref, f_ref, keep_ref, here_ref, back_ref, swap_ref,
    out_ref, coef_ref, side_ref,
    za_ref, zb_ref, left_ref, right_ref, inn_left_ref, inn_right_ref,
):
    _, odd, first_tile, last_tile = flags_of(code_ref)
    block = SWEEPS * OWN * LEV
    inner = TX * OWN * LEV

    def states(left, right):
        za_ref[0:block, :] = left[0:block, :]
        za_ref[block + inner : 2 * block + inner, :] = right[0:block, :]
        inn_left_ref[...] = left[N_INN:N_RATE, :]
        inn_right_ref[...] = right[N_INN:N_RATE, :]

    def rates(left, right):
        left_ref[...] = left[...]
        right_ref[...] = right[...]

    by_side(odd, states, here_ref, back_ref)
    by_side(odd, rates, here_ref.at[pl.ds(N_RATE, N_ROWS - N_RATE)], swap_ref)
    za_ref[block : block + inner, :] = keep_ref[0:inner, :]
    open_left = jnp.where(first_tile != 0, 0.0, 1.0)
    open_right = jnp.where(last_tile != 0, 0.0, 1.0)
    lane = lax.broadcasted_iota(jnp.int32, (8, NY), 1)
    sub = lax.broadcasted_iota(jnp.int32, (8, NY), 0)
    for at in range(XW):
        mixings = []

        def put(kind, at_row, value):
            coef_ref[kind * PLANE + at_row : kind * PLANE + at_row + 8, :] = value

        for half in range(2):
            fields = []
            for index in range(4):
                if HALO <= at < HALO + TX:
                    fields.append(column(keep_ref, K_RATE + index * STEP, at - HALO, half))
                else:
                    side, place = (left_ref, at) if at < HALO else (right_ref, at - HALO - TX)
                    row = (index * HALO + place) * LEV + 8 * half
                    fields.append(side[row : row + 8, :])
            diff, wind_x, wind_y, mixing = fields
            e_rate, w_rate = toward(diff, wind_x), against(diff, wind_x)
            n_rate, s_rate = toward(diff, wind_y), against(diff, wind_y)
            mixings.append(mixing)
            row = at * LEV + 8 * half
            put(0, row, 1.0 - (e_rate + w_rate + n_rate + s_rate + mixing + mixing))
            if at < XW - 1:
                put(1, row + LEV, e_rate * open_left if at == HALO - 1 else e_rate)
            if at > 0:
                put(2, row - LEV, w_rate * open_right if at == HALO + TX else w_rate)
            put(3, row, jnp.where(lane == 0, 0.0, pltpu.roll(n_rate, 1, 1)))
            put(4, row, jnp.where(lane == NY - 1, 0.0, pltpu.roll(s_rate, NY - 1, 1)))
        row = at * LEV
        down_low, down_high = pltpu.roll(mixings[0], 1, 0), pltpu.roll(mixings[1], 1, 0)
        put(5, row, jnp.where(sub == 0, 0.0, down_low))
        put(5, row + 8, jnp.where(sub == 0, down_low, down_high))
        up_low, up_high = pltpu.roll(mixings[0], 7, 0), pltpu.roll(mixings[1], 7, 0)
        put(6, row, jnp.where(sub == 7, up_high, up_low))
        put(6, row + 8, jnp.where(sub == 7, 0.0, up_high))
    edge = slice(N_EDGE - N_RATE, N_ROWS - N_RATE)
    coef_ref[PLANE : PLANE + LEV, :] = left_ref[edge, :]
    coef_ref[3 * PLANE - LEV : 3 * PLANE, :] = right_ref[edge, :]

    row_y = level_rows()

    def side_step(step):
        for index, (ref, columns) in enumerate(((inn_left_ref, LEFT), (inn_right_ref, RIGHT))):
            value = ref[pl.ds(pl.multiple_of((step - 1) * LEV, LEV), LEV), :]
            cell = ref[pl.ds(7 * LEV + step, 1), :].astype(jnp.int32)
            placed = place_forcing(value, cell, columns, row_y)
            side_ref[pl.ds(pl.multiple_of(step * STEP + index * HALO * LEV, LEV), HALO * LEV), :] = placed

    def side_steps(index, carry):
        for offset in range(2):
            side_step(2 + index * 2 + offset)
        return carry

    side_step(1)
    lax.fori_loop(0, 3, side_steps, 0)

    def rows_of_ref(ref):
        return lambda step, place: (ref, step * STEP + place * LEV)

    def store(chain, at, half, total):
        out_ref[pl.ds(chain * STEP + half * 8 * TX + at - SWEEPS, 8, stride=TX), :] = total

    sweeps(OWN, 0, za_ref, zb_ref, coef_ref, rows_of_ref(f_ref), rows_of_ref(side_ref), store)


def next_chains(part, code_ref, coef_ref, t_ref, here_ref, back_ref, za_ref, zb_ref, tails, sides, forcing, store):
    first_state, states, first_inn, inns = PARTS[part]
    last, odd = flags_of(code_ref)[:2]
    wrap, first, extra = factors(last)
    width = states * LEV
    tail = TAILS[part]

    def scaled(value):
        amounts = [first if first_state + slot == 0 else wrap for slot in range(states)]
        return [value[slot * LEV : slot * LEV + LEV, :] * amount for slot, amount in enumerate(amounts)]

    def fill(at, ref, base):
        for slot, value in enumerate(scaled(ref[base : base + width, :])):
            row = at * width + slot * LEV
            za_ref[row : row + LEV, :] = value

    def edges(left, right):
        for place in range(SWEEPS):
            fill(place, left, place * width)
            fill(SWEEPS + TX + place, right, tail + place * width)
        tails[0][...] = left[SWEEPS * width : SWEEPS * width + tail, :]
        tails[1][...] = right[0:tail, :]

    by_side(odd, edges, here_ref, back_ref)
    for col in range(TX):
        fill(SWEEPS + col, t_ref, T_BASE[part] + tail + col * width)

    row_y = level_rows()
    for slot in range(inns):
        for index, (ref, columns) in enumerate(zip(tails, (LEFT, RIGHT))):
            value = ref[slot * LEV : slot * LEV + LEV, :] * wrap
            row = inns * LEV + first_inn + slot
            cell = ref[row : row + 1, :].astype(jnp.int32)
            placed = place_forcing(value, cell, columns, row_y)
            start = slot * STEP + index * HALO * LEV
            sides[part][start : start + HALO * LEV, :] = placed

    if first_state == 0:

        @pl.when(last != 0)
        def _():
            def leave(left, right):
                for place in range(2 * HALO):
                    inside = place < HALO
                    ref, base = (left, (place + 1) * width) if inside else (right, tail + (place - HALO) * width)
                    rows = slice(place * LEV, place * LEV + LEV)
                    sides[part][rows, :] = sides[part][rows, :] - ref[base : base + LEV, :] * extra

            by_side(odd, leave, here_ref, back_ref)

    def own_rows(step, place):
        ref, base = (forcing[0], step) if step < STEPS_DEV else (forcing[1], step - STEPS_DEV)
        return ref, base * STEP + place * LEV

    def side_rows(step, place):
        if step < STEPS_DEV:
            return forcing[2], step * STEP + place * LEV
        part_of = 0 if step - STEPS_DEV < PARTS[1][2] else 1
        return sides[part_of], (step - STEPS_DEV - PARTS[part_of][2]) * STEP + place * LEV

    sweeps(states, OWN + first_state, za_ref, zb_ref, coef_ref, own_rows, side_rows, store)


def mid_kernel(
    code_ref, coef_ref, f_ref, fnext_ref, side_ref, t_ref, here_ref, back_ref,
    out_ref, side_out_ref,
    za_ref, zb_ref, tail_left_ref, tail_right_ref,
):
    def store(chain, at, half, total):
        out_ref[pl.ds(chain * STEP + half * 8 * TX + at - SWEEPS, 8, stride=TX), :] = total

    next_chains(
        0, code_ref, coef_ref, t_ref, here_ref, back_ref, za_ref, zb_ref, (tail_left_ref, tail_right_ref),
        (side_out_ref, None), (f_ref, fnext_ref, side_ref), store,
    )


def late_kernel(
    code_ref, early_ref, mid_ref, coef_ref, f_ref, fnext_ref, side_ref, side_mid_ref, t_ref, here_ref, back_ref,
    out_ref,
    za_ref, zb_ref, tail_left_ref, tail_right_ref, side_late_ref,
):
    begun = OWN + PARTS[0][1]
    out_ref[0 : OWN * STEP, :] = early_ref[...]
    out_ref[OWN * STEP : begun * STEP, :] = mid_ref[...]

    def store(chain, at, half, total):
        out_ref[pl.ds((begun + chain) * STEP + half * 8 * TX + at - SWEEPS, 8, stride=TX), :] = total

    next_chains(
        1, code_ref, coef_ref, t_ref, here_ref, back_ref, za_ref, zb_ref, (tail_left_ref, tail_right_ref),
        (side_mid_ref, side_late_ref), (f_ref, fnext_ref, side_ref), store,
    )


def vmem(count):
    return [pl.BlockSpec(memory_space=pltpu.VMEM)] * count


def rows_of(count):
    return jax.ShapeDtypeStruct((count, NY), jnp.float32)


def scratch(count):
    return pltpu.VMEM((count, NY), jnp.float32)


SMEM_SPEC = pl.BlockSpec(memory_space=pltpu.SMEM)


def update(adjoint_iterate, innovations, station_cells, diffusivity, wind_x, wind_y, vertical_mixing):
    time_parts = lax.axis_size("tm")
    tiles = lax.axis_size("space")
    lam = adjoint_iterate.reshape(STEPS_DEV * STEP, NY)
    inn = innovations.reshape(STEPS_DEV * LEV, NY)
    fields = [field.reshape(STEP, NY) for field in (diffusivity, wind_x, wind_y, vertical_mixing)]
    time_rank, tile = lax.axis_index("tm"), lax.axis_index("space")
    odd = time_rank & 1
    code = (time_rank == time_parts - 1) + 2 * odd + 4 * (tile == 0) + 8 * (tile == tiles - 1)
    code = code.astype(jnp.int32).reshape(1)

    ahead = [((i + 1) % time_parts, i) for i in range(time_parts)]

    def neighbours(flip):
        pairs = []
        for part in range(time_parts):
            step = 1 if part % 2 == flip else -1
            for place in range(tiles):
                inside = 0 <= place + step < tiles
                target = part * tiles + place + step if inside else (part ^ 1) * tiles + place
                pairs.append((part * tiles + place, target))
        return pairs

    there, again = neighbours(0), neighbours(1)
    both = ("tm", "space")
    partners = [(part, part ^ 1) for part in range(time_parts)]

    def kernel(function, inputs, outputs, scratches, flops):
        return pl.pallas_call(
            function,
            out_shape=tuple(rows_of(rows) for rows in outputs),
            in_specs=inputs,
            out_specs=tuple(vmem(len(outputs))),
            scratch_shapes=scratches,
            compiler_params=pltpu.CompilerParams(vmem_limit_bytes=12 << 20),
            cost_estimate=pl.CostEstimate(flops=flops, bytes_accessed=4_000_000, transcendentals=0),
        )

    arguments = (lam, inn, station_cells, *fields)
    pay_here, pay_back, pay_t, keep = kernel(
        pack_kernel,
        [SMEM_SPEC] + [pl.BlockSpec(memory_space=pltpu.HBM)] * 7,
        (N_ROWS, N_RATE, T_ROWS, K_ROWS),
        [
            scratch(STEPS_DEV * STEP),
            pltpu.VMEM(station_cells.shape, station_cells.dtype),
            pltpu.SemaphoreType.DMA((8,)),
        ],
        1_000_000,
    )(code, *[pltpu.with_memory_space_constraint(value, pltpu.HBM) for value in arguments])

    got_t = lax.ppermute(pay_t, "tm", ahead)
    here_one = lax.ppermute(pay_here, both, there)
    back_one = lax.ppermute(pay_back, both, again)
    parts = []
    for part in range(2):
        rows = part_rows(part)
        span = 2 * TAILS[part] + TX * PARTS[part][1] * LEV - rows
        up = span * (1 - odd)
        here = lax.dynamic_slice_in_dim(got_t, T_BASE[part] + up, rows)
        back = lax.dynamic_slice_in_dim(got_t, T_BASE[part] + span - up, rows)
        parts.append((lax.ppermute(here, both, there), lax.ppermute(back, both, again)))
    swapped = lax.ppermute(here_one[N_RATE:], "tm", partners)

    (forcing,) = kernel(own_kernel, vmem(1), (STEPS_DEV * STEP,), [], 5_000_000)(keep)
    (forcing_next,) = kernel(next_kernel, [SMEM_SPEC] + vmem(1), (FNEXT * STEP,), [], 3_000_000)(code, got_t)

    def states(count):
        return [scratch(ZW * count * LEV)] * 2

    out_early, coef, side = kernel(
        early_kernel,
        [SMEM_SPEC] + vmem(5),
        (OWN * STEP, 7 * PLANE, STEPS_DEV * STEP),
        states(OWN) + [scratch(N_ROWS - N_RATE)] * 2 + [scratch(N_RATE - N_INN)] * 2,
        10_000_000,
    )(code, forcing, keep, here_one, back_one, swapped)
    out_mid, side_mid = kernel(
        mid_kernel,
        [SMEM_SPEC] + vmem(7),
        (PARTS[0][1] * STEP, PARTS[0][3] * STEP),
        states(PARTS[0][1]) + [scratch(TAILS[0])] * 2,
        7_000_000,
    )(code, coef, forcing, forcing_next, side, got_t, *parts[0])
    (out,) = kernel(
        late_kernel,
        [SMEM_SPEC] + vmem(10),
        (STEPS_DEV * STEP,),
        states(PARTS[1][1]) + [scratch(TAILS[1])] * 2 + [scratch(PARTS[1][3] * STEP)],
        10_000_000,
    )(code, out_early, out_mid, coef, forcing, forcing_next, side, side_mid, got_t, *parts[1])
    return out.reshape(STEPS_DEV, LEV, TX, NY)


def solution(mesh):
    in_specs = (
        P("tm", None, "space", None),
        P("tm", None, "space"),
        P("tm", "space"),
        P(None, "space", None),
        P(None, "space", None),
        P(None, "space", None),
        P(None, "space", None),
    )
    out_specs = P("tm", None, "space", None)
    return jax.shard_map(update, mesh=mesh, in_specs=in_specs, out_specs=out_specs, check_vma=False)
```

```python
import jax
import jax.numpy as jnp
from jax import lax
from jax.experimental import pallas as pl
from jax.experimental.pallas import tpu as pltpu
from jax.sharding import PartitionSpec as P


LEV = 16
TX = 8
NY = 128
STEPS_DEV = 8
SWEEPS = 5
HALO = SWEEPS - 1
NEXT = SWEEPS
FNEXT = SWEEPS - 1
OWN = STEPS_DEV - NEXT
XW = TX + 2 * HALO
ZW = XW + 2
STEP = LEV * TX
PLANE = XW * LEV

circ_alpha = 0.1

PARTS = ((0, 2, 0, 1), (2, 3, 1, 3))
TAILS = tuple(part[3] * LEV + 8 for part in PARTS)
T_ROWS = tuple(2 * tail + TX * part[1] * LEV for part, tail in zip(PARTS, TAILS))
N_INN = SWEEPS * OWN * LEV
N_CELL = N_INN + 7 * LEV
N_RATE = N_CELL + 8
N_EDGE = N_RATE + 4 * HALO * LEV
N_ROWS = N_EDGE + LEV
K_INN = OWN * STEP
K_CELL = K_INN + STEPS_DEV * LEV
K_RATE = K_CELL + 8
K_ROWS = K_RATE + 4 * STEP


def part_rows(part):
    return SWEEPS * PARTS[part][1] * LEV + TAILS[part]


def toward(diff, wind):
    return diff + jnp.maximum(-wind, 0.0)


def against(diff, wind):
    return diff + jnp.maximum(wind, 0.0)


def column(ref, base, col, half):
    return ref[pl.ds(base + half * 8 * TX + col, 8, stride=TX), :]


def flags_of(code_ref):
    return [lax.shift_right_logical(code_ref[0], bit) & 1 for bit in range(4)]


def pack_kernel(
    code_ref, lam_hbm, inn_hbm, cell_hbm, diff_hbm, wx_hbm, wy_hbm, vm_hbm,
    here_ref, back_ref, ta_ref, tb_ref, keep_ref,
    lam_ref, cell_ref, sems,
):
    late, soon = pl.ds(NEXT * STEP, OWN * STEP), pl.ds(0, NEXT * STEP)
    pairs = [(lam_hbm.at[late], lam_ref.at[late])]
    pairs += [
        (rate, keep_ref.at[pl.ds(K_RATE + index * STEP, STEP)])
        for index, rate in enumerate((diff_hbm, wx_hbm, wy_hbm, vm_hbm))
    ]
    pairs += [(inn_hbm, keep_ref.at[pl.ds(K_INN, STEPS_DEV * LEV)]), (cell_hbm, cell_ref)]
    pairs += [(lam_hbm.at[soon], lam_ref.at[soon])]
    copies = [pltpu.make_async_copy(source, target, sems.at[index]) for index, (source, target) in enumerate(pairs)]
    for copy in copies:
        copy.start()
    odd = flags_of(code_ref)[1]
    far = TX - SWEEPS
    sides = ((here_ref, far * (1 - odd)), (back_ref, far * odd))
    copies[0].wait()
    for half in range(2):
        for col in range(TX):
            for slot in range(OWN):
                row = (col * OWN + slot) * LEV + 8 * half
                keep_ref[row : row + 8, :] = column(lam_ref, (NEXT + slot) * STEP, col, half)
    for ref, first in sides:
        start = pl.multiple_of(first * (OWN * LEV), LEV)
        ref[0:N_INN, :] = keep_ref[pl.ds(start, N_INN), :]
    for copy in copies[1:5]:
        copy.wait()
    first = sides[0][1]
    rate_first = (TX - HALO) * (1 - odd)
    for half in range(2):
        for index in range(4):
            for place in range(HALO):
                row = N_RATE + (index * HALO + place) * LEV + 8 * half
                here_ref[row : row + 8, :] = column(keep_ref, K_RATE + index * STEP, rate_first + place, half)
        leaving = toward(column(keep_ref, K_RATE, far, half), column(keep_ref, K_RATE + STEP, far, half))
        place = SWEEPS - 1
        entering = against(column(keep_ref, K_RATE, place, half), column(keep_ref, K_RATE + STEP, place, half))
        here_ref[N_EDGE + 8 * half : N_EDGE + 8 * half + 8, :] = jnp.where(odd == 0, leaving, entering)
    for copy in copies[5:7]:
        copy.wait()
    cells = cell_ref[...].astype(jnp.float32)
    keep_ref[K_CELL:K_RATE, :] = cells
    for ref in (here_ref, back_ref):
        ref[N_INN:N_CELL, :] = keep_ref[K_INN + LEV : K_INN + 8 * LEV, :]
        ref[N_CELL:N_RATE, :] = cells
    payloads = (ta_ref, tb_ref)
    for (_, states, first_inn, inns), tail, t_ref in zip(PARTS, TAILS, payloads):
        for start in (0, tail + TX * states * LEV):
            row = K_INN + first_inn * LEV
            t_ref[start : start + inns * LEV, :] = keep_ref[row : row + inns * LEV, :]
            t_ref[start + inns * LEV : start + tail, :] = cells
    copies[7].wait()
    for (first_state, states, _, _), tail, t_ref in zip(PARTS, TAILS, payloads):
        for half in range(2):
            for col in range(TX):
                for slot in range(states):
                    row = tail + (col * states + slot) * LEV + 8 * half
                    t_ref[row : row + 8, :] = column(lam_ref, (first_state + slot) * STEP, col, half)


def by_side(odd, work, here, back):
    pl.when(odd == 0)(lambda: work(here, back))
    pl.when(odd != 0)(lambda: work(back, here))


def place_forcing(value, cell, columns, row_y):
    cell_x = lax.shift_right_logical(cell, 7).astype(jnp.float32)
    cell_y = (cell & (NY - 1)).astype(jnp.float32)
    high = value.astype(jnp.bfloat16)
    rest = value - high.astype(jnp.float32)
    mid = rest.astype(jnp.bfloat16)
    low = (rest - mid.astype(jnp.float32)).astype(jnp.bfloat16)
    spread_x = jnp.broadcast_to(cell_x, (LEV, NY)).astype(jnp.bfloat16)
    spread_y = jnp.broadcast_to(cell_y, (LEV, NY)).astype(jnp.bfloat16)
    zero = jnp.zeros((LEV, NY), jnp.bfloat16)
    one = jnp.ones((LEV, NY), jnp.bfloat16)
    hot_y = jnp.concatenate(
        [jnp.where(row_y[LEV * part : LEV * part + LEV] == spread_y, one, zero) for part in range(NY // LEV)], axis=0
    )
    blocks = []
    for x in range(*columns):
        hot = spread_x == jnp.full((LEV, NY), x, jnp.bfloat16)
        blocks.append(jnp.concatenate([jnp.where(hot, part, zero) for part in (high, mid, low)], axis=1))
    return lax.dot_general(
        jnp.concatenate(blocks, axis=0),
        jnp.concatenate([hot_y, hot_y, hot_y], axis=1),
        (((1,), (1,)), ((), ())),
        preferred_element_type=jnp.float32,
    )


def level_rows():
    return lax.broadcasted_iota(jnp.int32, (NY, NY), 0).astype(jnp.float32).astype(jnp.bfloat16)


LEFT = (TX - HALO, TX)
RIGHT = (0, HALO)


def sweeps(chains, first_chain, za_ref, zb_ref, coef_ref, own_rows, side_rows, store):
    width = chains * LEV
    buffers = (za_ref, zb_ref)
    for sweep in range(SWEEPS):
        source, target = buffers[sweep % 2], buffers[(sweep + 1) % 2]

        def one_column(at, rows, place, source=source, target=target, sweep=sweep):
            base = at * width
            plane = (at - 1) * LEV
            for half in range(2):
                coef = [coef_ref[pl.ds(kind * PLANE + plane + 8 * half, 8), :] for kind in range(7)]
                for chain in range(chains):
                    row = base + chain * LEV + 8 * half
                    centre = source[pl.ds(row, 8), :]
                    step = first_chain + chain + HALO - sweep
                    ref, start = rows(step, place)
                    west_east = coef[1] * source[pl.ds(row - width, 8), :] + coef[2] * source[pl.ds(row + width, 8), :]
                    along = coef[3] * pltpu.roll(centre, 1, 1) + coef[4] * pltpu.roll(centre, NY - 1, 1)
                    down_up = coef[5] * source[pl.ds(row - 1, 8), :] + coef[6] * source[pl.ds(row + 1, 8), :]
                    total = ref[pl.ds(start + 8 * half, 8), :] + coef[0] * centre
                    total = ((total + west_east) + down_up) + along
                    if sweep < SWEEPS - 1:
                        target[pl.ds(row, 8), :] = total
                    else:
                        store(chain, at, half, total)

        for place in range(TX):
            one_column(SWEEPS + place, own_rows, place)
        for offset in range(HALO - sweep):
            one_column(SWEEPS - 1 - offset, side_rows, HALO - 1 - offset)
            one_column(SWEEPS + TX + offset, side_rows, HALO + offset)


def factors(last):
    last = last != 0
    return jnp.where(last, circ_alpha, 1.0), jnp.where(last, 0.0, 1.0), jnp.where(last, circ_alpha, 0.0)


def own_kernel(keep_ref, f_ref):
    row_y = level_rows()

    def own_steps(index, carry):
        for offset in range(4):
            step = index * 4 + offset
            value = keep_ref[pl.ds(pl.multiple_of(K_INN + step * LEV, LEV), LEV), :]
            cell = keep_ref[pl.ds(K_CELL + step, 1), :].astype(jnp.int32)
            placed = place_forcing(value, cell, (0, TX), row_y)
            f_ref[pl.ds(pl.multiple_of(step * STEP, STEP), STEP), :] = placed
        return carry

    lax.fori_loop(0, STEPS_DEV // 4, own_steps, 0)


def next_kernel(code_ref, ta_ref, tb_ref, f_ref):
    wrap, _, extra = factors(flags_of(code_ref)[0])
    row_y = level_rows()
    for (_, _, first_inn, inns), t_ref in zip(PARTS, (ta_ref, tb_ref)):
        for slot in range(inns):
            step = first_inn + slot
            value = t_ref[slot * LEV : slot * LEV + LEV, :] * wrap
            row = inns * LEV + step
            cell = t_ref[row : row + 1, :].astype(jnp.int32)
            placed = place_forcing(value, cell, (0, TX), row_y)
            if step == 0:
                width = PARTS[0][1] * LEV
                states = [t_ref[TAILS[0] + col * width : TAILS[0] + col * width + LEV, :] for col in range(TX)]
                placed = placed - jnp.concatenate(states, axis=0) * extra
            f_ref[step * STEP : step * STEP + STEP, :] = placed


def early_kernel(
    code_ref, f_ref, keep_ref, here_ref, back_ref, swap_ref,
    out_ref, coef_ref, side_ref,
    za_ref, zb_ref, left_ref, right_ref, inn_left_ref, inn_right_ref,
):
    _, odd, first_tile, last_tile = flags_of(code_ref)
    block = SWEEPS * OWN * LEV
    inner = TX * OWN * LEV

    def states(left, right):
        za_ref[0:block, :] = left[0:block, :]
        za_ref[block + inner : 2 * block + inner, :] = right[0:block, :]
        inn_left_ref[...] = left[N_INN:N_RATE, :]
        inn_right_ref[...] = right[N_INN:N_RATE, :]

    def rates(left, right):
        left_ref[...] = left[...]
        right_ref[...] = right[...]

    by_side(odd, states, here_ref, back_ref)
    by_side(odd, rates, here_ref.at[pl.ds(N_RATE, N_ROWS - N_RATE)], swap_ref)
    za_ref[block : block + inner, :] = keep_ref[0:inner, :]
    open_left = jnp.where(first_tile != 0, 0.0, 1.0)
    open_right = jnp.where(last_tile != 0, 0.0, 1.0)
    lane = lax.broadcasted_iota(jnp.int32, (8, NY), 1)
    sub = lax.broadcasted_iota(jnp.int32, (8, NY), 0)
    for at in range(XW):
        mixings = []

        def put(kind, at_row, value):
            coef_ref[kind * PLANE + at_row : kind * PLANE + at_row + 8, :] = value

        for half in range(2):
            fields = []
            for index in range(4):
                if HALO <= at < HALO + TX:
                    fields.append(column(keep_ref, K_RATE + index * STEP, at - HALO, half))
                else:
                    side, place = (left_ref, at) if at < HALO else (right_ref, at - HALO - TX)
                    row = (index * HALO + place) * LEV + 8 * half
                    fields.append(side[row : row + 8, :])
            diff, wind_x, wind_y, mixing = fields
            e_rate, w_rate = toward(diff, wind_x), against(diff, wind_x)
            n_rate, s_rate = toward(diff, wind_y), against(diff, wind_y)
            mixings.append(mixing)
            row = at * LEV + 8 * half
            put(0, row, 1.0 - (e_rate + w_rate + n_rate + s_rate + mixing + mixing))
            if at < XW - 1:
                put(1, row + LEV, e_rate * open_left if at == HALO - 1 else e_rate)
            if at > 0:
                put(2, row - LEV, w_rate * open_right if at == HALO + TX else w_rate)
            put(3, row, jnp.where(lane == 0, 0.0, pltpu.roll(n_rate, 1, 1)))
            put(4, row, jnp.where(lane == NY - 1, 0.0, pltpu.roll(s_rate, NY - 1, 1)))
        row = at * LEV
        down_low, down_high = pltpu.roll(mixings[0], 1, 0), pltpu.roll(mixings[1], 1, 0)
        put(5, row, jnp.where(sub == 0, 0.0, down_low))
        put(5, row + 8, jnp.where(sub == 0, down_low, down_high))
        up_low, up_high = pltpu.roll(mixings[0], 7, 0), pltpu.roll(mixings[1], 7, 0)
        put(6, row, jnp.where(sub == 7, up_high, up_low))
        put(6, row + 8, jnp.where(sub == 7, 0.0, up_high))
    edge = slice(N_EDGE - N_RATE, N_ROWS - N_RATE)
    coef_ref[PLANE : PLANE + LEV, :] = left_ref[edge, :]
    coef_ref[3 * PLANE - LEV : 3 * PLANE, :] = right_ref[edge, :]

    row_y = level_rows()

    def side_step(step):
        for index, (ref, columns) in enumerate(((inn_left_ref, LEFT), (inn_right_ref, RIGHT))):
            value = ref[pl.ds(pl.multiple_of((step - 1) * LEV, LEV), LEV), :]
            cell = ref[pl.ds(7 * LEV + step, 1), :].astype(jnp.int32)
            placed = place_forcing(value, cell, columns, row_y)
            side_ref[pl.ds(pl.multiple_of(step * STEP + index * HALO * LEV, LEV), HALO * LEV), :] = placed

    def side_steps(index, carry):
        for offset in range(2):
            side_step(2 + index * 2 + offset)
        return carry

    side_step(1)
    lax.fori_loop(0, 3, side_steps, 0)

    def rows_of_ref(ref):
        return lambda step, place: (ref, step * STEP + place * LEV)

    def store(chain, at, half, total):
        out_ref[pl.ds(chain * STEP + half * 8 * TX + at - SWEEPS, 8, stride=TX), :] = total

    sweeps(OWN, 0, za_ref, zb_ref, coef_ref, rows_of_ref(f_ref), rows_of_ref(side_ref), store)


def next_chains(part, code_ref, coef_ref, t_ref, here_ref, back_ref, za_ref, zb_ref, tails, sides, forcing, store):
    first_state, states, first_inn, inns = PARTS[part]
    last, odd = flags_of(code_ref)[:2]
    wrap, first, extra = factors(last)
    width = states * LEV
    tail = TAILS[part]

    def scaled(value):
        amounts = [first if first_state + slot == 0 else wrap for slot in range(states)]
        return [value[slot * LEV : slot * LEV + LEV, :] * amount for slot, amount in enumerate(amounts)]

    def fill(at, ref, base):
        for slot, value in enumerate(scaled(ref[base : base + width, :])):
            row = at * width + slot * LEV
            za_ref[row : row + LEV, :] = value

    def edges(left, right):
        for place in range(SWEEPS):
            fill(place, left, place * width)
            fill(SWEEPS + TX + place, right, tail + place * width)
        tails[0][...] = left[SWEEPS * width : SWEEPS * width + tail, :]
        tails[1][...] = right[0:tail, :]

    by_side(odd, edges, here_ref, back_ref)
    for col in range(TX):
        fill(SWEEPS + col, t_ref, tail + col * width)

    row_y = level_rows()
    for slot in range(inns):
        for index, (ref, columns) in enumerate(zip(tails, (LEFT, RIGHT))):
            value = ref[slot * LEV : slot * LEV + LEV, :] * wrap
            row = inns * LEV + first_inn + slot
            cell = ref[row : row + 1, :].astype(jnp.int32)
            placed = place_forcing(value, cell, columns, row_y)
            start = slot * STEP + index * HALO * LEV
            sides[part][start : start + HALO * LEV, :] = placed

    if first_state == 0:

        @pl.when(last != 0)
        def _():
            def leave(left, right):
                for place in range(2 * HALO):
                    inside = place < HALO
                    ref, base = (left, (place + 1) * width) if inside else (right, tail + (place - HALO) * width)
                    rows = slice(place * LEV, place * LEV + LEV)
                    sides[part][rows, :] = sides[part][rows, :] - ref[base : base + LEV, :] * extra

            by_side(odd, leave, here_ref, back_ref)

    def own_rows(step, place):
        ref, base = (forcing[0], step) if step < STEPS_DEV else (forcing[1], step - STEPS_DEV)
        return ref, base * STEP + place * LEV

    def side_rows(step, place):
        if step < STEPS_DEV:
            return forcing[2], step * STEP + place * LEV
        part_of = 0 if step - STEPS_DEV < PARTS[1][2] else 1
        return sides[part_of], (step - STEPS_DEV - PARTS[part_of][2]) * STEP + place * LEV

    sweeps(states, OWN + first_state, za_ref, zb_ref, coef_ref, own_rows, side_rows, store)


def mid_kernel(
    code_ref, coef_ref, f_ref, fnext_ref, side_ref, t_ref, here_ref, back_ref,
    out_ref, side_out_ref,
    za_ref, zb_ref, tail_left_ref, tail_right_ref,
):
    def store(chain, at, half, total):
        out_ref[pl.ds(chain * STEP + half * 8 * TX + at - SWEEPS, 8, stride=TX), :] = total

    next_chains(
        0, code_ref, coef_ref, t_ref, here_ref, back_ref, za_ref, zb_ref, (tail_left_ref, tail_right_ref),
        (side_out_ref, None), (f_ref, fnext_ref, side_ref), store,
    )


def late_kernel(
    code_ref, early_ref, mid_ref, coef_ref, f_ref, fnext_ref, side_ref, side_mid_ref, t_ref, here_ref, back_ref,
    out_ref,
    za_ref, zb_ref, tail_left_ref, tail_right_ref, side_late_ref,
):
    begun = OWN + PARTS[0][1]
    out_ref[0 : OWN * STEP, :] = early_ref[...]
    out_ref[OWN * STEP : begun * STEP, :] = mid_ref[...]

    def store(chain, at, half, total):
        out_ref[pl.ds((begun + chain) * STEP + half * 8 * TX + at - SWEEPS, 8, stride=TX), :] = total

    next_chains(
        1, code_ref, coef_ref, t_ref, here_ref, back_ref, za_ref, zb_ref, (tail_left_ref, tail_right_ref),
        (side_mid_ref, side_late_ref), (f_ref, fnext_ref, side_ref), store,
    )


def vmem(count):
    return [pl.BlockSpec(memory_space=pltpu.VMEM)] * count


def rows_of(count):
    return jax.ShapeDtypeStruct((count, NY), jnp.float32)


def scratch(count):
    return pltpu.VMEM((count, NY), jnp.float32)


SMEM_SPEC = pl.BlockSpec(memory_space=pltpu.SMEM)


def update(adjoint_iterate, innovations, station_cells, diffusivity, wind_x, wind_y, vertical_mixing):
    time_parts = lax.axis_size("tm")
    tiles = lax.axis_size("space")
    lam = adjoint_iterate.reshape(STEPS_DEV * STEP, NY)
    inn = innovations.reshape(STEPS_DEV * LEV, NY)
    fields = [field.reshape(STEP, NY) for field in (diffusivity, wind_x, wind_y, vertical_mixing)]
    time_rank, tile = lax.axis_index("tm"), lax.axis_index("space")
    odd = time_rank & 1
    code = (time_rank == time_parts - 1) + 2 * odd + 4 * (tile == 0) + 8 * (tile == tiles - 1)
    code = code.astype(jnp.int32).reshape(1)

    ahead = [((i + 1) % time_parts, i) for i in range(time_parts)]

    def neighbours(flip):
        pairs = []
        for part in range(time_parts):
            step = 1 if part % 2 == flip else -1
            for place in range(tiles):
                inside = 0 <= place + step < tiles
                target = part * tiles + place + step if inside else (part ^ 1) * tiles + place
                pairs.append((part * tiles + place, target))
        return pairs

    there, again = neighbours(0), neighbours(1)
    both = ("tm", "space")
    partners = [(part, part ^ 1) for part in range(time_parts)]

    def kernel(function, inputs, outputs, scratches, flops):
        return pl.pallas_call(
            function,
            out_shape=tuple(rows_of(rows) for rows in outputs),
            in_specs=inputs,
            out_specs=tuple(vmem(len(outputs))),
            scratch_shapes=scratches,
            compiler_params=pltpu.CompilerParams(vmem_limit_bytes=12 << 20),
            cost_estimate=pl.CostEstimate(flops=flops, bytes_accessed=4_000_000, transcendentals=0),
        )

    arguments = (lam, inn, station_cells, *fields)
    pay_here, pay_back, pay_ta, pay_tb, keep = kernel(
        pack_kernel,
        [SMEM_SPEC] + [pl.BlockSpec(memory_space=pltpu.HBM)] * 7,
        (N_ROWS, N_RATE, *T_ROWS, K_ROWS),
        [
            scratch(STEPS_DEV * STEP),
            pltpu.VMEM(station_cells.shape, station_cells.dtype),
            pltpu.SemaphoreType.DMA((8,)),
        ],
        1_000_000,
    )(code, *[pltpu.with_memory_space_constraint(value, pltpu.HBM) for value in arguments])

    got_ta = lax.ppermute(pay_ta, "tm", ahead)
    here_one = lax.ppermute(pay_here, both, there)
    back_one = lax.ppermute(pay_back, both, again)
    got_tb = lax.ppermute(pay_tb, "tm", ahead)
    parts = []
    for part, got_t in enumerate((got_ta, got_tb)):
        rows = part_rows(part)
        span = T_ROWS[part] - rows
        up = span * (1 - odd)
        here = lax.dynamic_slice_in_dim(got_t, up, rows)
        back = lax.dynamic_slice_in_dim(got_t, span - up, rows)
        parts.append((lax.ppermute(here, both, there), lax.ppermute(back, both, again)))
    swapped = lax.ppermute(here_one[N_RATE:], "tm", partners)

    (forcing,) = kernel(own_kernel, vmem(1), (STEPS_DEV * STEP,), [], 5_000_000)(keep)
    (forcing_next,) = kernel(next_kernel, [SMEM_SPEC] + vmem(2), (FNEXT * STEP,), [], 3_000_000)(code, got_ta, got_tb)

    def states(count):
        return [scratch(ZW * count * LEV)] * 2

    out_early, coef, side = kernel(
        early_kernel,
        [SMEM_SPEC] + vmem(5),
        (OWN * STEP, 7 * PLANE, STEPS_DEV * STEP),
        states(OWN) + [scratch(N_ROWS - N_RATE)] * 2 + [scratch(N_RATE - N_INN)] * 2,
        10_000_000,
    )(code, forcing, keep, here_one, back_one, swapped)
    out_mid, side_mid = kernel(
        mid_kernel,
        [SMEM_SPEC] + vmem(7),
        (PARTS[0][1] * STEP, PARTS[0][3] * STEP),
        states(PARTS[0][1]) + [scratch(TAILS[0])] * 2,
        7_000_000,
    )(code, coef, forcing, forcing_next, side, got_ta, *parts[0])
    (out,) = kernel(
        late_kernel,
        [SMEM_SPEC] + vmem(10),
        (STEPS_DEV * STEP,),
        states(PARTS[1][1]) + [scratch(TAILS[1])] * 2 + [scratch(PARTS[1][3] * STEP)],
        10_000_000,
    )(code, out_early, out_mid, coef, forcing, forcing_next, side, side_mid, got_tb, *parts[1])
    return out.reshape(STEPS_DEV, LEV, TX, NY)


def solution(mesh):
    in_specs = (
        P("tm", None, "space", None),
        P("tm", None, "space"),
        P("tm", "space"),
        P(None, "space", None),
        P(None, "space", None),
        P(None, "space", None),
        P(None, "space", None),
    )
    out_specs = P("tm", None, "space", None)
    return jax.shard_map(update, mesh=mesh, in_specs=in_specs, out_specs=out_specs, check_vma=False)
```

```python
import jax
import jax.numpy as jnp
from jax import lax
from jax.experimental import pallas as pl
from jax.experimental.pallas import tpu as pltpu
from jax.sharding import PartitionSpec as P


LEV = 16
TX = 8
NY = 128
STEPS_DEV = 8
SWEEPS = 5
HALO = SWEEPS - 1
NEXT = SWEEPS
FNEXT = SWEEPS - 1
OWN = STEPS_DEV - NEXT
XW = TX + 2 * HALO
ZW = XW + 2
STEP = LEV * TX
PLANE = XW * LEV

circ_alpha = 0.1


PARTS = ((0, 3), (3, 2))
TAILS = (FNEXT * LEV + 8, 0)
T_ROWS = tuple(tail + TX * part[1] * LEV for part, tail in zip(PARTS, TAILS))
N_INN = SWEEPS * OWN * LEV
N_CELL = N_INN + 7 * LEV
N_RATE = N_CELL + 8
N_EDGE = N_RATE + 4 * HALO * LEV
N_ROWS = N_EDGE + LEV
K_INN = OWN * STEP
K_CELL = K_INN + STEPS_DEV * LEV
K_RATE = K_CELL + 8
K_ROWS = K_RATE + 4 * STEP


def part_rows(part):
    return SWEEPS * PARTS[part][1] * LEV + TAILS[part]


def part_column(part, place, shift=0):
    row = (place - shift) * PARTS[part][1] * LEV
    return row if place < SWEEPS else row + TAILS[part]


def toward(diff, wind):
    return diff + jnp.maximum(-wind, 0.0)


def against(diff, wind):
    return diff + jnp.maximum(wind, 0.0)


def column(ref, base, col, half):
    return ref[pl.ds(base + half * 8 * TX + col, 8, stride=TX), :]


def flags_of(code_ref):
    return [lax.shift_right_logical(code_ref[0], bit) & 1 for bit in range(4)]


def pack_kernel(
    code_ref, lam_hbm, inn_hbm, cell_hbm, diff_hbm, wx_hbm, wy_hbm, vm_hbm,
    here_ref, back_ref, ta_ref, tb_ref, keep_ref,
    lam_ref, cell_ref, sems,
):
    late, soon = pl.ds(NEXT * STEP, OWN * STEP), pl.ds(0, NEXT * STEP)
    pairs = [(lam_hbm.at[late], lam_ref.at[late])]
    pairs += [
        (rate, keep_ref.at[pl.ds(K_RATE + index * STEP, STEP)])
        for index, rate in enumerate((diff_hbm, wx_hbm, wy_hbm, vm_hbm))
    ]
    pairs += [(inn_hbm, keep_ref.at[pl.ds(K_INN, STEPS_DEV * LEV)]), (cell_hbm, cell_ref)]
    pairs += [(lam_hbm.at[soon], lam_ref.at[soon])]
    copies = [pltpu.make_async_copy(source, target, sems.at[index]) for index, (source, target) in enumerate(pairs)]
    for copy in copies:
        copy.start()
    odd = flags_of(code_ref)[1]
    far = TX - SWEEPS
    sides = ((here_ref, far * (1 - odd)), (back_ref, far * odd))
    copies[0].wait()
    for half in range(2):
        for col in range(TX):
            for slot in range(OWN):
                row = (col * OWN + slot) * LEV + 8 * half
                keep_ref[row : row + 8, :] = column(lam_ref, (NEXT + slot) * STEP, col, half)
    for ref, first in sides:
        start = pl.multiple_of(first * (OWN * LEV), LEV)
        ref[0:N_INN, :] = keep_ref[pl.ds(start, N_INN), :]
    for copy in copies[1:5]:
        copy.wait()
    first = sides[0][1]
    rate_first = (TX - HALO) * (1 - odd)
    for half in range(2):
        for index in range(4):
            for place in range(HALO):
                row = N_RATE + (index * HALO + place) * LEV + 8 * half
                here_ref[row : row + 8, :] = column(keep_ref, K_RATE + index * STEP, rate_first + place, half)
        leaving = toward(column(keep_ref, K_RATE, far, half), column(keep_ref, K_RATE + STEP, far, half))
        place = SWEEPS - 1
        entering = against(column(keep_ref, K_RATE, place, half), column(keep_ref, K_RATE + STEP, place, half))
        here_ref[N_EDGE + 8 * half : N_EDGE + 8 * half + 8, :] = jnp.where(odd == 0, leaving, entering)
    for copy in copies[5:7]:
        copy.wait()
    cells = cell_ref[...].astype(jnp.float32)
    keep_ref[K_CELL:K_RATE, :] = cells
    for ref in (here_ref, back_ref):
        ref[N_INN:N_CELL, :] = keep_ref[K_INN + LEV : K_INN + 8 * LEV, :]
        ref[N_CELL:N_RATE, :] = cells
    start = part_column(0, SWEEPS) - TAILS[0]
    ta_ref[start : start + FNEXT * LEV, :] = keep_ref[K_INN : K_INN + FNEXT * LEV, :]
    ta_ref[start + FNEXT * LEV : start + TAILS[0], :] = cells
    copies[7].wait()
    for part, ref in enumerate((ta_ref, tb_ref)):
        first_state, states = PARTS[part]
        for half in range(2):
            for col in range(TX):
                for slot in range(states):
                    row = part_column(part, col) + slot * LEV + 8 * half
                    ref[row : row + 8, :] = column(lam_ref, (first_state + slot) * STEP, col, half)


def by_side(odd, work, here, back):
    pl.when(odd == 0)(lambda: work(here, back))
    pl.when(odd != 0)(lambda: work(back, here))


def place_forcing(value, cell, columns, row_y):
    cell_x = lax.shift_right_logical(cell, 7).astype(jnp.float32)
    cell_y = (cell & (NY - 1)).astype(jnp.float32)
    high = value.astype(jnp.bfloat16)
    rest = value - high.astype(jnp.float32)
    mid = rest.astype(jnp.bfloat16)
    low = (rest - mid.astype(jnp.float32)).astype(jnp.bfloat16)
    spread_x = jnp.broadcast_to(cell_x, (LEV, NY)).astype(jnp.bfloat16)
    spread_y = jnp.broadcast_to(cell_y, (LEV, NY)).astype(jnp.bfloat16)
    zero = jnp.zeros((LEV, NY), jnp.bfloat16)
    one = jnp.ones((LEV, NY), jnp.bfloat16)
    hot_y = jnp.concatenate(
        [jnp.where(row_y[LEV * part : LEV * part + LEV] == spread_y, one, zero) for part in range(NY // LEV)], axis=0
    )
    hots = [spread_x == jnp.full((LEV, NY), x, jnp.bfloat16) for x in range(*columns)]
    placed = lax.dot_general(
        jnp.concatenate([jnp.where(hot, part, zero) for part in (high, mid, low) for hot in hots], axis=0),
        hot_y,
        (((1,), (1,)), ((), ())),
        preferred_element_type=jnp.float32,
    )
    rows = len(hots) * LEV
    return placed[0:rows] + (placed[rows : 2 * rows] + placed[2 * rows : 3 * rows])


def level_rows():
    return lax.broadcasted_iota(jnp.int32, (NY, NY), 0).astype(jnp.float32).astype(jnp.bfloat16)


LEFT = (TX - HALO, TX)
RIGHT = (0, HALO)


def sweeps(chains, first_chain, za_ref, zb_ref, coef_ref, own_rows, side_rows, store, finish=None):
    width = chains * LEV
    buffers = (za_ref, zb_ref)
    for sweep in range(SWEEPS):
        source, target = buffers[sweep % 2], buffers[(sweep + 1) % 2]

        def one_column(at, rows, place, halves=(0, 1), source=source, target=target, sweep=sweep):
            base = at * width
            plane = (at - 1) * LEV
            for half in halves:
                coef = [coef_ref[pl.ds(kind * PLANE + plane + 8 * half, 8), :] for kind in range(7)]
                for chain in range(chains):
                    row = base + chain * LEV + 8 * half
                    centre = source[pl.ds(row, 8), :]
                    step = first_chain + chain + HALO - sweep
                    ref, start = rows(step, place)
                    west_east = coef[1] * source[pl.ds(row - width, 8), :] + coef[2] * source[pl.ds(row + width, 8), :]
                    along = coef[3] * pltpu.roll(centre, 1, 1) + coef[4] * pltpu.roll(centre, NY - 1, 1)
                    down_up = coef[5] * source[pl.ds(row - 1, 8), :] + coef[6] * source[pl.ds(row + 1, 8), :]
                    total = ref[pl.ds(start + 8 * half, 8), :] + coef[0] * centre
                    total = ((total + west_east) + down_up) + along
                    if sweep < SWEEPS - 1:
                        target[pl.ds(row, 8), :] = total
                    else:
                        store(chain, at, half, total)

        if sweep == SWEEPS - 1 and finish is not None:
            for half in range(2):
                for place in range(TX):
                    one_column(SWEEPS + place, own_rows, place, (half,))
                finish(half)
            break
        for place in range(TX):
            one_column(SWEEPS + place, own_rows, place)
        for offset in range(HALO - sweep):
            one_column(SWEEPS - 1 - offset, side_rows, HALO - 1 - offset)
            one_column(SWEEPS + TX + offset, side_rows, HALO + offset)


def factors(last):
    last = last != 0
    return jnp.where(last, circ_alpha, 1.0), jnp.where(last, 0.0, 1.0), jnp.where(last, circ_alpha, 0.0)


def own_kernel(keep_ref, f_ref):
    row_y = level_rows()

    for step in range(STEPS_DEV):
        value = keep_ref[K_INN + step * LEV : K_INN + step * LEV + LEV, :]
        cell = keep_ref[K_CELL + step : K_CELL + step + 1, :].astype(jnp.int32)
        f_ref[step * STEP : step * STEP + STEP, :] = place_forcing(value, cell, (0, TX), row_y)


def next_kernel(code_ref, ta_ref, f_ref):
    wrap, _, extra = factors(flags_of(code_ref)[0])
    row_y = level_rows()
    base = part_column(0, SWEEPS) - TAILS[0]
    for step in range(FNEXT):
        value = ta_ref[base + step * LEV : base + step * LEV + LEV, :] * wrap
        row = base + FNEXT * LEV + step
        cell = ta_ref[row : row + 1, :].astype(jnp.int32)
        placed = place_forcing(value, cell, (0, TX), row_y)
        if step == 0:
            states = [ta_ref[part_column(0, col) : part_column(0, col) + LEV, :] for col in range(TX)]
            placed = placed - jnp.concatenate(states, axis=0) * extra
        f_ref[step * STEP : step * STEP + STEP, :] = placed


def side_kernel(code_ref, here_ref, back_ref, side_ref, left_ref, right_ref):
    odd = flags_of(code_ref)[1]

    def forcing(left, right):
        left_ref[...] = left[N_INN:N_RATE, :]
        right_ref[...] = right[N_INN:N_RATE, :]

    by_side(odd, forcing, here_ref, back_ref)
    row_y = level_rows()

    for step in range(1, STEPS_DEV):
        for index, (ref, columns) in enumerate(((left_ref, LEFT), (right_ref, RIGHT))):
            value = ref[(step - 1) * LEV : step * LEV, :]
            cell = ref[7 * LEV + step : 7 * LEV + step + 1, :].astype(jnp.int32)
            placed = place_forcing(value, cell, columns, row_y)
            start = step * STEP + index * HALO * LEV
            side_ref[start : start + HALO * LEV, :] = placed


def early_kernel(
    code_ref, f_ref, keep_ref, here_ref, back_ref, swap_ref, side_ref,
    out_ref, coef_ref,
    za_ref, zb_ref, left_ref, right_ref,
):
    _, odd, first_tile, last_tile = flags_of(code_ref)
    block = SWEEPS * OWN * LEV
    inner = TX * OWN * LEV

    def states(left, right):
        za_ref[0:block, :] = left[0:block, :]
        za_ref[block + inner : 2 * block + inner, :] = right[0:block, :]

    def rates(left, right):
        left_ref[...] = left[...]
        right_ref[...] = right[...]

    by_side(odd, states, here_ref, back_ref)
    by_side(odd, rates, here_ref.at[pl.ds(N_RATE, N_ROWS - N_RATE)], swap_ref)
    za_ref[block : block + inner, :] = keep_ref[0:inner, :]
    open_left = jnp.where(first_tile != 0, 0.0, 1.0)
    open_right = jnp.where(last_tile != 0, 0.0, 1.0)
    lane = lax.broadcasted_iota(jnp.int32, (8, NY), 1)
    sub = lax.broadcasted_iota(jnp.int32, (8, NY), 0)
    for at in range(XW):
        mixings = []

        def put(kind, at_row, value):
            coef_ref[kind * PLANE + at_row : kind * PLANE + at_row + 8, :] = value

        for half in range(2):
            fields = []
            for index in range(4):
                if HALO <= at < HALO + TX:
                    fields.append(column(keep_ref, K_RATE + index * STEP, at - HALO, half))
                else:
                    side, place = (left_ref, at) if at < HALO else (right_ref, at - HALO - TX)
                    row = (index * HALO + place) * LEV + 8 * half
                    fields.append(side[row : row + 8, :])
            diff, wind_x, wind_y, mixing = fields
            e_rate, w_rate = toward(diff, wind_x), against(diff, wind_x)
            n_rate, s_rate = toward(diff, wind_y), against(diff, wind_y)
            mixings.append(mixing)
            row = at * LEV + 8 * half
            put(0, row, 1.0 - (e_rate + w_rate + n_rate + s_rate + mixing + mixing))
            if at < XW - 1:
                put(1, row + LEV, e_rate * open_left if at == HALO - 1 else e_rate)
            if at > 0:
                put(2, row - LEV, w_rate * open_right if at == HALO + TX else w_rate)
            put(3, row, jnp.where(lane == 0, 0.0, pltpu.roll(n_rate, 1, 1)))
            put(4, row, jnp.where(lane == NY - 1, 0.0, pltpu.roll(s_rate, NY - 1, 1)))
        row = at * LEV
        down_low, down_high = pltpu.roll(mixings[0], 1, 0), pltpu.roll(mixings[1], 1, 0)
        put(5, row, jnp.where(sub == 0, 0.0, down_low))
        put(5, row + 8, jnp.where(sub == 0, down_low, down_high))
        up_low, up_high = pltpu.roll(mixings[0], 7, 0), pltpu.roll(mixings[1], 7, 0)
        put(6, row, jnp.where(sub == 7, up_high, up_low))
        put(6, row + 8, jnp.where(sub == 7, 0.0, up_high))
    edge = slice(N_EDGE - N_RATE, N_ROWS - N_RATE)
    coef_ref[PLANE : PLANE + LEV, :] = left_ref[edge, :]
    coef_ref[3 * PLANE - LEV : 3 * PLANE, :] = right_ref[edge, :]

    def rows_of_ref(ref):
        return lambda step, place: (ref, step * STEP + place * LEV)

    def store(chain, at, half, total):
        out_ref[pl.ds(chain * STEP + half * 8 * TX + at - SWEEPS, 8, stride=TX), :] = total

    sweeps(OWN, 0, za_ref, zb_ref, coef_ref, rows_of_ref(f_ref), rows_of_ref(side_ref), store)


def next_states(part, code_ref, t_ref, here_ref, back_ref, za_ref, tails):
    first_state, states = PARTS[part]
    last, odd = flags_of(code_ref)[:2]
    wrap, first, _ = factors(last)
    width = states * LEV

    def fill(at, ref, base):
        for slot in range(states):
            row = at * width + slot * LEV
            amount = first if first_state + slot == 0 else wrap
            za_ref[row : row + LEV, :] = ref[base + slot * LEV : base + slot * LEV + LEV, :] * amount

    far = TX - SWEEPS

    def edges(left, right):
        for place in range(SWEEPS):
            fill(place, left, part_column(part, far + place, far))
            fill(SWEEPS + TX + place, right, part_column(part, place))
        if tails:
            start = part_column(part, SWEEPS, far) - TAILS[part]
            tails[0][...] = left[start : start + TAILS[part], :]
            start = part_column(part, SWEEPS) - TAILS[part]
            tails[1][...] = right[start : start + TAILS[part], :]

    by_side(odd, edges, here_ref, back_ref)
    for col in range(TX):
        fill(SWEEPS + col, t_ref, part_column(part, col))


def either(ref, next_ref):
    def rows(step, place):
        chosen, base = (ref, step) if step < STEPS_DEV else (next_ref, step - STEPS_DEV)
        return chosen, base * STEP + place * LEV

    return rows


def mid_kernel(
    code_ref, coef_ref, f_ref, fnext_ref, side_ref, t_ref, here_ref, back_ref,
    out_ref, side_next_ref,
    za_ref, zb_ref, tail_left_ref, tail_right_ref,
):
    tails = (tail_left_ref, tail_right_ref)
    next_states(0, code_ref, t_ref, here_ref, back_ref, za_ref, tails)
    last, odd = flags_of(code_ref)[:2]
    wrap, _, extra = factors(last)
    row_y = level_rows()
    for step in range(FNEXT):
        for index, (ref, columns) in enumerate(zip(tails, (LEFT, RIGHT))):
            value = ref[step * LEV : step * LEV + LEV, :] * wrap
            cell = ref[FNEXT * LEV + step : FNEXT * LEV + step + 1, :].astype(jnp.int32)
            placed = place_forcing(value, cell, columns, row_y)
            start = step * STEP + index * HALO * LEV
            side_next_ref[start : start + HALO * LEV, :] = placed

    @pl.when(last != 0)
    def _():
        far = TX - SWEEPS

        def leave(left, right):
            for place in range(2 * HALO):
                if place < HALO:
                    ref, base = left, part_column(0, far + place + 1, far)
                else:
                    ref, base = right, part_column(0, place - HALO)
                rows = slice(place * LEV, place * LEV + LEV)
                side_next_ref[rows, :] = side_next_ref[rows, :] - ref[base : base + LEV, :] * extra

        by_side(odd, leave, here_ref, back_ref)

    def store(chain, at, half, total):
        out_ref[pl.ds(chain * STEP + half * 8 * TX + at - SWEEPS, 8, stride=TX), :] = total

    rows = [either(f_ref, fnext_ref), either(side_ref, side_next_ref)]
    sweeps(PARTS[0][1], OWN, za_ref, zb_ref, coef_ref, *rows, store)


def late_kernel(
    code_ref, early_ref, mid_ref, coef_ref, f_ref, fnext_ref, side_ref, side_next_ref, t_ref, here_ref, back_ref,
    out_hbm,
    za_ref, zb_ref, out_ref, sems,
):
    begun = OWN + PARTS[0][1]
    chains = PARTS[1][1]
    copies = [
        pltpu.make_async_copy(early_ref, out_hbm.at[pl.ds(0, OWN * STEP)], sems.at[0]),
        pltpu.make_async_copy(mid_ref, out_hbm.at[pl.ds(OWN * STEP, PARTS[0][1] * STEP)], sems.at[1]),
    ]
    for copy in copies:
        copy.start()
    next_states(1, code_ref, t_ref, here_ref, back_ref, za_ref, ())

    def store(chain, at, half, total):
        out_ref[pl.ds(chain * STEP + half * 8 * TX + at - SWEEPS, 8, stride=TX), :] = total

    def finish(half):
        for chain in range(chains):
            rows = pl.ds(chain * STEP + half * 8 * TX, 8 * TX)
            target = out_hbm.at[pl.ds((begun + chain) * STEP + half * 8 * TX, 8 * TX)]
            copy = pltpu.make_async_copy(out_ref.at[rows], target, sems.at[2 + half * chains + chain])
            copy.start()
            copies.append(copy)

    rows = [either(f_ref, fnext_ref), either(side_ref, side_next_ref)]
    sweeps(chains, begun, za_ref, zb_ref, coef_ref, *rows, store, finish)
    for copy in copies:
        copy.wait()


def vmem(count):
    return [pl.BlockSpec(memory_space=pltpu.VMEM)] * count


def rows_of(count):
    return jax.ShapeDtypeStruct((count, NY), jnp.float32)


def scratch(count):
    return pltpu.VMEM((count, NY), jnp.float32)


SMEM_SPEC = pl.BlockSpec(memory_space=pltpu.SMEM)


def update(adjoint_iterate, innovations, station_cells, diffusivity, wind_x, wind_y, vertical_mixing):
    time_parts = lax.axis_size("tm")
    tiles = lax.axis_size("space")
    lam = adjoint_iterate.reshape(STEPS_DEV * STEP, NY)
    inn = innovations.reshape(STEPS_DEV * LEV, NY)
    fields = [field.reshape(STEP, NY) for field in (diffusivity, wind_x, wind_y, vertical_mixing)]
    time_rank, tile = lax.axis_index("tm"), lax.axis_index("space")
    odd = time_rank & 1
    code = (time_rank == time_parts - 1) + 2 * odd + 4 * (tile == 0) + 8 * (tile == tiles - 1)
    code = code.astype(jnp.int32).reshape(1)

    ahead = [((i + 1) % time_parts, i) for i in range(time_parts)]

    def neighbours(flip):
        pairs = []
        for part in range(time_parts):
            step = 1 if part % 2 == flip else -1
            for place in range(tiles):
                inside = 0 <= place + step < tiles
                target = part * tiles + place + step if inside else (part ^ 1) * tiles + place
                pairs.append((part * tiles + place, target))
        return pairs

    there, again = neighbours(0), neighbours(1)
    both = ("tm", "space")
    partners = [(part, part ^ 1) for part in range(time_parts)]

    def kernel(function, inputs, outputs, scratches, flops, out_space=pltpu.VMEM):
        return pl.pallas_call(
            function,
            out_shape=tuple(rows_of(rows) for rows in outputs),
            in_specs=inputs,
            out_specs=tuple(pl.BlockSpec(memory_space=out_space) for _ in outputs),
            scratch_shapes=scratches,
            compiler_params=pltpu.CompilerParams(vmem_limit_bytes=12 << 20),
            cost_estimate=pl.CostEstimate(flops=flops, bytes_accessed=4_000_000, transcendentals=0),
        )

    arguments = (lam, inn, station_cells, *fields)
    pay_here, pay_back, pay_ta, pay_tb, keep = kernel(
        pack_kernel,
        [SMEM_SPEC] + [pl.BlockSpec(memory_space=pltpu.HBM)] * 7,
        (N_ROWS, N_RATE, *T_ROWS, K_ROWS),
        [
            scratch(STEPS_DEV * STEP),
            pltpu.VMEM(station_cells.shape, station_cells.dtype),
            pltpu.SemaphoreType.DMA((8,)),
        ],
        1_000_000,
    )(code, *[pltpu.with_memory_space_constraint(value, pltpu.HBM) for value in arguments])

    got_ta = lax.ppermute(pay_ta, "tm", ahead)
    here_one = lax.ppermute(pay_here, both, there)
    back_one = lax.ppermute(pay_back, both, again)
    got_tb = lax.ppermute(pay_tb, "tm", ahead)
    parts = []
    for part, got_t in enumerate((got_ta, got_tb)):
        rows = part_rows(part)
        span = T_ROWS[part] - rows
        up = span * (1 - odd)
        here = lax.dynamic_slice_in_dim(got_t, up, rows)
        back = lax.dynamic_slice_in_dim(got_t, span - up, rows)
        parts.append((lax.ppermute(here, both, there), lax.ppermute(back, both, again)))
    swapped = lax.ppermute(here_one[N_RATE:], "tm", partners)

    (forcing,) = kernel(own_kernel, vmem(1), (STEPS_DEV * STEP,), [], 5_000_000)(keep)
    (forcing_next,) = kernel(next_kernel, [SMEM_SPEC] + vmem(1), (FNEXT * STEP,), [], 3_000_000)(code, got_ta)
    (side,) = kernel(
        side_kernel, [SMEM_SPEC] + vmem(2), (STEPS_DEV * STEP,), [scratch(N_RATE - N_INN)] * 2, 5_000_000
    )(code, here_one, back_one)

    def states(count):
        return [scratch(ZW * count * LEV)] * 2

    out_early, coef = kernel(
        early_kernel,
        [SMEM_SPEC] + vmem(6),
        (OWN * STEP, 7 * PLANE),
        states(OWN) + [scratch(N_ROWS - N_RATE)] * 2,
        10_000_000,
    )(code, forcing, keep, here_one, back_one, swapped, side)
    out_mid, side_next = kernel(
        mid_kernel,
        [SMEM_SPEC] + vmem(7),
        (PARTS[0][1] * STEP, FNEXT * STEP),
        states(PARTS[0][1]) + [scratch(TAILS[0])] * 2,
        7_000_000,
    )(code, coef, forcing, forcing_next, side, got_ta, *parts[0])
    (out,) = kernel(
        late_kernel,
        [SMEM_SPEC] + vmem(10),
        (STEPS_DEV * STEP,),
        states(PARTS[1][1]) + [scratch(PARTS[1][1] * STEP), pltpu.SemaphoreType.DMA((2 + 2 * PARTS[1][1],))],
        10_000_000,
        pl.ANY,
    )(code, out_early, out_mid, coef, forcing, forcing_next, side, side_next, got_tb, *parts[1])
    return out.reshape(STEPS_DEV, LEV, TX, NY)


def solution(mesh):
    in_specs = (
        P("tm", None, "space", None),
        P("tm", None, "space"),
        P("tm", "space"),
        P(None, "space", None),
        P(None, "space", None),
        P(None, "space", None),
        P(None, "space", None),
    )
    out_specs = P("tm", None, "space", None)
    return jax.shard_map(update, mesh=mesh, in_specs=in_specs, out_specs=out_specs, check_vma=False)
```
